256 devices in a mesh: cell: 32 (over y_hi, z, core), brick: 8 (over x, y_lo).
Axes of the slice: x: 4, y: 4 (y_hi: 2, y_lo: 2; y = y_hi * 2 + y_lo), z: 8, core: 2. Of those that a mesh axis runs over, the one named last changes fastest.
Arguments:
- features: bfloat16 [32, 8, 128, 256], P('cell', 'brick'), may hold values from -6 to 6
- species: int32 [32, 8, 128], P('cell', 'brick'), may hold values from 0 to 3
- species_table: bfloat16 [4, 256], replicated, may hold values from -3 to 3
- neighbours: int32 [32, 8, 64, 128], P('cell', 'brick'), may hold values from 0 to 383
- counts: int32 [32, 8, 128], P('cell', 'brick'), may hold values from 1 to 64
- send_lists: int32 [32, 8, 8, 32], P('cell', 'brick'), may hold values from 0 to 127
- distances: float32 [32, 8, 64, 128], P('cell', 'brick'), may hold values from 0.05 to 1
- head_decay: float32 [8], replicated, may hold values from 0.25 to 4
- norm_gain: float32 [256], replicated, may hold values from 0.5 to 1.5
- readout: float32 [256], replicated, may hold values from -0.375 to 0.375
- targets: float32 [32, 8, 128], P('cell', 'brick'), may hold values from -6 to 6
- master: float32 [4, 256, 256], P(None, 'cell'), as said below
- moment: float32 [4, 256, 256], P(None, 'cell'), may hold values from -3 to 3
- second: float32 [4, 256, 256], P(None, 'cell'), may hold values from 0.1 to 1
Outputs:
- energies: float32 [32, 8, 128], P('cell', 'brick')
- moment_new: float32 [4, 256, 256], P(None, 'cell')
- second_new: float32 [4, 256, 256], P(None, 'cell')
- adam_step: float32 [4, 256, 256], P(None, 'cell')
The draws below stay inside these ranges and needn't reach their ends.
Inputs may be any that keep to these rules, and one draw needn't show every extreme that they name: `master`: projection entries lie within -48 * 256^-0.5 and 48 * 256^-0.5.
All inputs are finite; a program needn't handle non-finite values.
Results may differ from the reference program's by a relative error of at most 0.0045.
The reference program's roundings to bfloat16 on the way count: a program that leaves them out, or rounds other values in their place, can miss the bound.
Values may be sent and summed in bfloat16 or wider, within the bound.
A program may use at most 64 MiB of HBM per device.

```python
import math
import jax
import jax.numpy as jnp
from jax import lax

C = 256
HEADS = 8
K = 64
TILE = 128
SPECIES = 4
ATOMS_DEV = 128
GHOST_SLOT = 32
CELLS = 32
BRICK_COUNT = 8
TABLE = 384


def draw_master(key, part):
    base_draw = jax.random.normal(key, (4, C, C), jnp.float32)
    base_draw = jnp.clip(base_draw, -6.0, 6.0) * (1.0 / math.sqrt(C))
    return base_draw


def with_ends(array, key, smallest, top_value):
    place = [jax.random.randint(jax.random.fold_in(key, axis), (), 0, length) for axis, length in enumerate(array.shape)]
    widest = array.shape.index(max(array.shape))
    next_to = place[:widest] + [(place[widest] + 1) % array.shape[widest]] + place[widest + 1:]
    return array.at[tuple(place)].set(smallest).at[tuple(next_to)].set(top_value)


def block_levels(stream_key, extent, split, smallest, high):
    loudness = 1.0
    for axis_at, shards_of in split:
        draws = jax.random.uniform(jax.random.fold_in(jax.random.fold_in(stream_key, 6), axis_at), (shards_of,), jnp.float32, smallest / len(split), high / len(split))
        loudness = loudness * jnp.repeat(jnp.exp(draws), extent[axis_at] // shards_of).reshape((-1,) + (1,) * (len(extent) - 1 - axis_at))
    return loudness


def centred(rng, extent, width, most, shards=(), kind=jnp.bfloat16):
    result = jax.random.normal(rng, extent, jnp.float32) * width
    if len(shards) > 0:
        result = block_levels(rng, extent, shards, -0.22, 0.18) * result
    return jnp.clip(result, min=-most, max=most).astype(kind)


def setup_inputs(seed: int = 0) -> dict:
    splits = jax.random.split(jax.random.key(seed), 15)
    features = centred(splits[0], (CELLS, BRICK_COUNT, ATOMS_DEV, C), 1.0, 6.0, ((0, 32), (1, 8)))
    species = with_ends(jax.random.randint(splits[1], (CELLS, BRICK_COUNT, ATOMS_DEV), 0, SPECIES), jax.random.fold_in(splits[1], 1), 0, SPECIES - 1).astype(jnp.int32)
    species_table = centred(splits[2], (SPECIES, C), 0.5, 3.0)
    neighbours = with_ends(jax.random.randint(splits[3], (CELLS, BRICK_COUNT, K, ATOMS_DEV), 0, TABLE), jax.random.fold_in(splits[3], 1), 0, TABLE - 1).astype(jnp.int32)
    counts = with_ends(jax.random.randint(splits[4], (CELLS, BRICK_COUNT, ATOMS_DEV), 1, K + 1), jax.random.fold_in(splits[4], 1), 1, K).astype(jnp.int32)
    send_lists = with_ends(jax.random.randint(splits[5], (CELLS, BRICK_COUNT, BRICK_COUNT, GHOST_SLOT), 0, ATOMS_DEV), jax.random.fold_in(splits[5], 1), 0, ATOMS_DEV - 1).astype(jnp.int32)
    distances = jnp.clip(0.05 + 0.95 * jax.random.uniform(splits[6], (CELLS, BRICK_COUNT, K, ATOMS_DEV), jnp.float32) ** block_levels(splits[6], (CELLS, BRICK_COUNT, K, ATOMS_DEV), ((0, 32), (1, 8)), -0.2, 0.2), 0.05, 1.0)
    head_decay = jnp.clip(jnp.exp(jax.random.uniform(splits[7], (HEADS,), jnp.float32, math.log(0.25), math.log(4.0))), 0.25, 4.0)
    norm_gain = jnp.clip(1.0 + 0.1 * jax.random.normal(splits[8], (C,), jnp.float32), 0.5, 1.5)
    readout = centred(splits[9], (C,), 0.0625, 0.375, (), jnp.float32)
    targets = centred(splits[10], (CELLS, BRICK_COUNT, ATOMS_DEV), 1.0, 6.0, ((0, 32), (1, 8)), jnp.float32)
    master = draw_master(jax.random.fold_in(splits[14], 71), 0)
    moment = centred(splits[12], (4, C, C), 0.5, 3.0, ((1, 32),), jnp.float32)
    second = jnp.clip(jnp.exp(math.log(1.0) - 2.3025851 * jax.random.uniform(splits[13], (4, C, C), jnp.float32) ** block_levels(splits[13], (4, C, C), ((1, 32),), -0.2, 0.2)), 0.1, 1.0)
    return dict(features=features, species=species, species_table=species_table, neighbours=neighbours, counts=counts, send_lists=send_lists, distances=distances, head_decay=head_decay, norm_gain=norm_gain, readout=readout, targets=targets, master=master, moment=moment, second=second)


loss_weight = 0.0625
epsilon_norm = 1e-06

def silu_slope(inputs):
    sigmoid_val = jax.nn.sigmoid(inputs)
    return sigmoid_val * (1.0 + inputs * (1.0 - sigmoid_val))

def normalize(embedded, norm_gain):
    rms_scale = lax.rsqrt(lax.optimization_barrier(jnp.mean(embedded * embedded, axis=-1, keepdims=True)) + epsilon_norm)
    return (embedded * rms_scale * norm_gain).astype(jnp.bfloat16)

def brick_sweep(query, key_table, value_table, embedded, neighbour_rows, local_count, local_dist, local_target, out_proj, head_decay, readout):
    atom_count, model_width = query.shape
    head_count = head_decay.shape[0]
    head_size = model_width // head_count
    slot_count = neighbour_rows.shape[0]
    score_scale = 1.0 / math.sqrt(head_size)
    table_rows = key_table.shape[0]

    def tile_step(grad_carry, tile_index):
        key_grads, value_grads = grad_carry
        row_start = (tile_index * TILE).astype(jnp.int32)
        query_tile = lax.dynamic_slice_in_dim(query, row_start, TILE, 0)
        nbr_tile = lax.dynamic_slice_in_dim(neighbour_rows, row_start, TILE, 1)
        count_tile = lax.dynamic_slice_in_dim(local_count, row_start, TILE, 0)
        dist_tile = lax.dynamic_slice_in_dim(local_dist, row_start, TILE, 1)
        embed_tile = lax.dynamic_slice_in_dim(embedded, row_start, TILE, 0)
        target_tile = lax.dynamic_slice_in_dim(local_target, row_start, TILE, 0)
        key_rows = key_table[nbr_tile].reshape(slot_count, TILE, head_count, head_size)
        value_rows = value_table[nbr_tile].reshape(slot_count, TILE, head_count, head_size)
        query_heads = query_tile.reshape(TILE, head_count, head_size)
        is_valid = (jnp.arange(slot_count)[:, None] < count_tile[None, :])[:, :, None]
        score = jnp.einsum('ahd,kahd->kah', query_heads.astype(jnp.float32), key_rows.astype(jnp.float32)) * score_scale
        score = score - head_decay[None, None, :] * dist_tile[:, :, None]
        score = jnp.where(is_valid, score, -1e+30)
        row_max = lax.optimization_barrier(jnp.max(score, axis=0, keepdims=True))
        exp_terms = jnp.where(is_valid, jnp.exp(score - row_max), 0.0)
        attention = exp_terms / lax.optimization_barrier(jnp.sum(exp_terms, axis=0, keepdims=True))
        attention_half = attention.astype(jnp.bfloat16)
        attended = jnp.einsum('kah,kahd->ahd', attention_half.astype(jnp.float32), value_rows.astype(jnp.float32))
        attended = attended.astype(jnp.bfloat16).reshape(TILE, model_width)
        updated = embed_tile + jnp.dot(attended, out_proj, preferred_element_type=jnp.float32)
        energy = lax.optimization_barrier(jnp.sum(readout * jax.nn.silu(updated), axis=-1))
        grad_energy = loss_weight * (energy - target_tile)
        grad_updated = (grad_energy[:, None] * readout * silu_slope(updated)).astype(jnp.bfloat16)
        grad_attended = jnp.dot(grad_updated, out_proj.T, preferred_element_type=jnp.float32).astype(jnp.bfloat16)
        grad_att_heads = grad_attended.reshape(TILE, head_count, head_size)
        grad_weights = jnp.einsum('ahd,kahd->kah', grad_att_heads.astype(jnp.float32), value_rows.astype(jnp.float32))
        grad_score = attention * (grad_weights - lax.optimization_barrier(jnp.sum(attention * grad_weights, axis=0, keepdims=True)))
        grad_score = grad_score.astype(jnp.bfloat16)
        grad_query = jnp.einsum('kah,kahd->ahd', grad_score.astype(jnp.float32), key_rows.astype(jnp.float32)) * score_scale
        grad_query = grad_query.astype(jnp.bfloat16).reshape(TILE, model_width)
        key_edge = grad_score.astype(jnp.float32)[..., None] * query_heads.astype(jnp.float32)[None] * score_scale
        value_edge = attention_half.astype(jnp.float32)[..., None] * grad_att_heads.astype(jnp.float32)[None]
        flattened_rows = nbr_tile.reshape(-1)
        key_grads = key_grads.at[flattened_rows].add(key_edge.reshape(-1, model_width))
        value_grads = value_grads.at[flattened_rows].add(value_edge.reshape(-1, model_width))
        return ((key_grads, value_grads), (energy, attended, grad_updated, grad_query))
    start_grads = (jnp.zeros((table_rows, model_width), jnp.float32), jnp.zeros((table_rows, model_width), jnp.float32))
    (key_grads, value_grads), stacked = lax.scan(tile_step, start_grads, jnp.arange(atom_count // TILE).astype(jnp.int32))
    energy, attended, grad_updated, grad_query = stacked
    return (key_grads, value_grads, energy.reshape(atom_count), attended.reshape(atom_count, model_width), grad_updated.reshape(atom_count, model_width), grad_query.reshape(atom_count, model_width))

def partial_owner(owner_sum, table_grads):

    def applied(peer):
        return owner_sum(table_grads, peer)
    return applied

def reference(features, species, species_table, neighbours, counts, send_lists, distances, head_decay, norm_gain, readout, targets, master, moment, second):
    attention_weights = master.astype(jnp.bfloat16)
    bricks = features.shape[1]
    atom_count = features.shape[2]
    model_width = features.shape[3]
    ghost_position = send_lists.shape[-1]

    def per_cell(grad_total, cell_inputs):
        cell_feat, cell_species, cell_nbr, cell_count, cell_send, cell_dist, cell_target = cell_inputs
        embedded = cell_feat.astype(jnp.float32) + species_table[cell_species].astype(jnp.float32)
        normed_features = normalize(embedded, norm_gain)
        flat_norm = normed_features.reshape(-1, model_width)
        query = jnp.dot(flat_norm, attention_weights[0], preferred_element_type=jnp.float32).astype(jnp.bfloat16).reshape(bricks, atom_count, model_width)
        key_all = jnp.dot(flat_norm, attention_weights[1], preferred_element_type=jnp.float32).astype(jnp.bfloat16).reshape(bricks, atom_count, model_width)
        value_all = jnp.dot(flat_norm, attention_weights[2], preferred_element_type=jnp.float32).astype(jnp.bfloat16).reshape(bricks, atom_count, model_width)

        def build_table(source_rows, brick_index):
            ghost_rows = source_rows[jnp.arange(bricks)[:, None], cell_send[:, brick_index, :]]
            return jnp.concatenate([source_rows[brick_index], ghost_rows.reshape(-1, model_width)], axis=0)

        def one_brick(brick_index):
            return brick_sweep(query[brick_index], build_table(key_all, brick_index), build_table(value_all, brick_index), embedded[brick_index], cell_nbr[brick_index], cell_count[brick_index], cell_dist[brick_index], cell_target[brick_index], attention_weights[3], head_decay, readout)
        key_grads, value_grads, energy, attended, grad_updated, grad_query = lax.map(one_brick, jnp.arange(bricks))

        def owner_sum(table_grads, peer):
            local_portion = table_grads[peer, :atom_count]
            ghost_part = table_grads[:, atom_count:].reshape(bricks, bricks, ghost_position, model_width)[:, peer]
            return local_portion.at[cell_send[peer].reshape(-1)].add(ghost_part.reshape(-1, model_width))
        grad_key = jax.vmap(partial_owner(owner_sum, key_grads))(jnp.arange(bricks)).astype(jnp.bfloat16)
        grad_value = jax.vmap(partial_owner(owner_sum, value_grads))(jnp.arange(bricks)).astype(jnp.bfloat16)
        norm_f = normed_features.astype(jnp.float32)
        grad_q = jnp.einsum('bac,bad->cd', norm_f, grad_query.astype(jnp.float32))
        key_gradient = jnp.einsum('bac,bad->cd', norm_f, grad_key.astype(jnp.float32))
        grad_v = jnp.einsum('bac,bad->cd', norm_f, grad_value.astype(jnp.float32))
        grad_o = jnp.einsum('bac,bad->cd', attended.astype(jnp.float32), grad_updated.astype(jnp.float32))
        return (grad_total + jnp.stack([grad_q, key_gradient, grad_v, grad_o]), energy)
    start_total = jnp.zeros((4, model_width, model_width), jnp.float32)
    grads, energies = lax.scan(per_cell, start_total, (features, species, neighbours, counts, send_lists, distances, targets))
    moment_new = 0.9 * moment + 0.1 * grads
    second_new = 0.999 * second + 0.001 * grads * grads
    adam_step = moment_new / (jnp.sqrt(second_new) + 1e-08)
    return (energies, moment_new, second_new, adam_step)
```

```python
import functools
import math

import jax
import jax.numpy as jnp
from jax import lax
from jax.experimental import pallas as pl
from jax.experimental.pallas import tpu as pltpu
from jax.sharding import PartitionSpec as P

MESH = pl.DeviceIdType.MESH
loss_weight = 0.0625
epsilon_norm = 1e-06
C = 256
H = 8
A = 128
K = 64
T = 384
CELLS = 32
BRICKS = 8
f32 = jnp.float32
bf16 = jnp.bfloat16


def dot(a, b, dims):
    return lax.dot_general(a, b, (dims, ((), ())), preferred_element_type=f32)


NN = ((1,), (0,))
NT = ((1,), (1,))
TN = ((0,), (0,))


def spread_kernel(feat, spec, table, sends, gain, master, emb, nt, wg, parcel, ssem, rsem, fsem, gsem):
    c = lax.axis_index("cell")
    b = lax.axis_index("brick")
    partner = c + 1 - 2 * lax.rem(c, 2)
    barrier = pltpu.get_barrier_semaphore()
    for k in range(1, 16):
        pl.semaphore_signal(barrier, inc=1, device_id={"cell": lax.rem(c + 2 * k, CELLS), "brick": b}, device_id_type=MESH)
    pl.semaphore_signal(barrier, inc=1, device_id={"cell": partner, "brick": b}, device_id_type=MESH)
    for d in range(1, 8):
        pl.semaphore_signal(barrier, inc=1, device_id={"cell": c, "brick": lax.rem(b + d, BRICKS)}, device_id_type=MESH)
    wg[c] = master[...].reshape(32, C).astype(bf16)

    eye = lax.broadcasted_iota(jnp.int32, (A, A), 0) == lax.broadcasted_iota(jnp.int32, (A, A), 1)
    col = jnp.sum(jnp.where(eye, jnp.broadcast_to(spec[...], (A, A)), 0).astype(f32), axis=1, keepdims=True)
    e = feat[...].astype(f32)
    tab = table[...].astype(f32)
    add = jnp.zeros((A, C), f32)
    for s in range(4):
        add = jnp.where(col == float(s), tab[s : s + 1, :], add)
    e = e + add
    emb[...] = e
    scale = lax.rsqrt(jnp.sum(e * e, axis=1, keepdims=True) * (1.0 / C) + epsilon_norm)
    n = (e * scale * gain[...]).astype(bf16)
    nt[0:A, :] = n
    row_id = lax.broadcasted_iota(jnp.int32, (A, 32), 0)
    for d in range(BRICKS):
        pick = (row_id == sends[d : d + 1, :]).astype(f32).astype(bf16)
        parcel[d] = dot(pick, n, TN).astype(bf16)
    nt[pl.ds(pl.multiple_of(A + 32 * b, 32), 32), :] = parcel[b]
    pl.semaphore_wait(barrier, 23)

    copies = []
    for k in range(1, 16):
        cp = pltpu.make_async_remote_copy(
            src_ref=wg.at[c], dst_ref=wg.at[c], send_sem=ssem.at[k], recv_sem=rsem.at[k],
            device_id={"cell": lax.rem(c + 2 * k, CELLS), "brick": b}, device_id_type=MESH)
        cp.start()
        copies.append(cp)
    ghosts = []
    for d in range(1, 8):
        cp = pltpu.make_async_remote_copy(
            src_ref=parcel.at[lax.rem(b + d, BRICKS)],
            dst_ref=nt.at[pl.ds(pl.multiple_of(A + 32 * b, 32), 32), :],
            send_sem=gsem.at[0, d], recv_sem=gsem.at[1, d],
            device_id={"cell": c, "brick": lax.rem(b + d, BRICKS)}, device_id_type=MESH)
        cp.start()
        ghosts.append(cp)
    forwards = []
    for k in range(16):
        if k:
            copies[k - 1].wait_recv()
        owner = lax.rem(c - 2 * k + CELLS, CELLS)
        cp = pltpu.make_async_remote_copy(
            src_ref=wg.at[owner], dst_ref=wg.at[owner], send_sem=fsem.at[0, k], recv_sem=fsem.at[1, k],
            device_id={"cell": partner, "brick": b}, device_id_type=MESH)
        cp.start()
        forwards.append(cp)
    for cp in ghosts:
        cp.wait()
    for cp in copies:
        cp.wait_send()
    for cp in forwards:
        cp.wait()


def spread(feat, spec, table, sends, gain, master):
    vm = pl.BlockSpec(memory_space=pltpu.VMEM)
    return pl.pallas_call(
        spread_kernel,
        out_shape=(
            jax.ShapeDtypeStruct((A, C), f32),
            jax.ShapeDtypeStruct((T, C), bf16),
            jax.ShapeDtypeStruct((CELLS, 32, C), bf16),
        ),
        in_specs=[vm] * 6,
        out_specs=(vm, vm, vm),
        scratch_shapes=[
            pltpu.VMEM((BRICKS, 32, C), bf16),
            pltpu.SemaphoreType.DMA((16,)),
            pltpu.SemaphoreType.DMA((16,)),
            pltpu.SemaphoreType.DMA((2, 16)),
            pltpu.SemaphoreType.DMA((2, 8)),
        ],
        compiler_params=pltpu.CompilerParams(collective_id=0, has_side_effects=True),
        name="spread",
    )(feat, spec, table, sends, gain, master)


def split(x):
    hi = x.astype(bf16)
    return hi, (x - hi.astype(f32)).astype(bf16)


def attend_kernel(emb, nt, wg, nbr, cnt, dist, decay, readout, target,
                  energy, grads,
                  idx, dst8, rep, qm, gm, big, att, lmat, onehot, pt_hi, pt_lo, idx2):
    scale = 1.0 / math.sqrt(C // H)

    def weight(m):
        return wg[:, 8 * m : 8 * m + 8, :].astype(f32).reshape(C, C).astype(bf16)

    w_q, w_k, w_v, w_o = weight(0), weight(1), weight(2), weight(3)
    n_all = nt[...]
    n_own = nt[0:A, :]
    q = dot(n_own, w_q, NN).astype(bf16)
    k = dot(n_all, w_k, NN).astype(bf16)
    v = dot(n_all, w_v, NN).astype(bf16)

    slot = lax.broadcasted_iota(jnp.int32, (K, A), 0)
    masked = jnp.where(slot < cnt[...], nbr[...], 512)
    m_t = masked.T
    d_t = dist[...].T
    m2 = jnp.concatenate([m_t, m_t], axis=1)
    d2 = jnp.concatenate([d_t, d_t], axis=1)
    idx2[...] = m2
    q32 = q.astype(f32)
    for h in range(H):
        idx[pl.ds(h, A, stride=8), :] = m2
        dst8[pl.ds(h, A, stride=8), :] = d2
        rep[pl.ds(h, A, stride=8), :] = q32[:, 0:128]
        rep[pl.ds(A * H + h, A, stride=8), :] = q32[:, 128:256]

    rows = A * H
    head_of_lane = lax.broadcasted_iota(jnp.int32, (rows, C), 1) // 32
    head_of_row = lax.rem(lax.broadcasted_iota(jnp.int32, (rows, C), 0), 8)
    head_mask = head_of_lane == head_of_row

    def spread_heads():
        x = jnp.concatenate([rep[0:rows, :], rep[rows : 2 * rows, :]], axis=1)
        return jnp.where(head_mask, x, 0.0).astype(bf16)

    qm[...] = spread_heads()
    big[...] = dot(qm[...], k, NT)

    lane = lax.broadcasted_iota(jnp.int32, (A, 128), 1)
    row_in = lax.broadcasted_iota(jnp.int32, (A, 128), 0)
    sub_head = lax.rem(row_in, 8)
    dec = jnp.zeros((A, 128), f32)
    for h in range(H):
        dec = jnp.where(sub_head == h, decay[h], dec)
    diag = lax.rem(row_in // 8, 2) == lane // 64
    t_row = lax.broadcasted_iota(jnp.int32, (T, 128), 0)
    lmat[...] = jnp.zeros((128, 1024), bf16)
    lane8 = lax.broadcasted_iota(jnp.int32, (8, 128), 1)

    def pick(s):
        r0 = pl.multiple_of(s * 128, 128)
        ix = idx[pl.ds(r0, 128), :]
        low = jnp.bitwise_and(ix, 127)
        blk = ix // 128
        out = jnp.zeros((128, 128), f32)
        for t in range(3):
            g = jnp.take_along_axis(big[pl.ds(r0, 128), 128 * t : 128 * t + 128], low, axis=1)
            out = jnp.where(blk == t, g, out)
        return out, ix < 512

    def scatter(s, w16):
        w32 = jnp.where(diag, w16.astype(f32), 0.0).astype(bf16)
        for t in range(8):
            lmat[16 * t : 16 * t + 16, 128 * t : 128 * t + 128] = w32[16 * t : 16 * t + 16, :]
        p = dot(onehot[s], lmat[...], NT)
        hi, lo = split(p)
        c0 = pl.multiple_of(s * 128, 128)
        pt_hi[:, pl.ds(c0, 128)] = hi
        pt_lo[:, pl.ds(c0, 128)] = lo

    @pl.loop(0, 8)
    def _(s):
        ev = idx2[pl.ds(16 * s, 8, stride=2), :]
        od = idx2[pl.ds(16 * s + 1, 8, stride=2), :]
        pair = jnp.where(lane8 < 64, ev, od)
        for t in range(8):
            hit = t_row == pair[t : t + 1, :]
            onehot[s, :, 128 * t : 128 * t + 128] = jnp.where(hit, 1.0, 0.0).astype(bf16)

    @pl.loop(0, 8)
    def _(s):
        r0 = pl.multiple_of(s * 128, 128)
        got, ok = pick(s)
        score = got * scale - dec * dst8[pl.ds(r0, 128), :]
        score = jnp.where(ok, score, -1e30)
        top = jnp.max(score, axis=1, keepdims=True)
        ex = jnp.where(ok, jnp.exp(score - top), 0.0)
        a = ex / (jnp.sum(ex, axis=1, keepdims=True) * 0.5)
        att[pl.ds(r0, 128), :] = a
        scatter(s, a.astype(bf16))

    lane_r = lax.broadcasted_iota(jnp.int32, (C, rows), 1)
    head_sel = lax.rem(lane_r, 8) == lax.broadcasted_iota(jnp.int32, (C, rows), 0) // 32
    collect = (lax.broadcasted_iota(jnp.int32, (A, rows), 1) // 8
               == lax.broadcasted_iota(jnp.int32, (A, rows), 0)).astype(f32).astype(bf16)

    def gather_heads(table_t, mult):
        full = dot(table_t, pt_hi[...], NN) + dot(table_t, pt_lo[...], NN)
        if mult is not None:
            full = full * mult
        kept = jnp.where(head_sel, full, 0.0).astype(bf16)
        return dot(collect, kept, NT).astype(bf16)

    attended = gather_heads(v.astype(f32).T.astype(bf16), None)
    updated = emb[...] + dot(attended, w_o, NN)
    sig = jax.nn.sigmoid(updated)
    e_col = jnp.sum(readout[...] * (updated * sig), axis=1, keepdims=True)
    eye = lax.broadcasted_iota(jnp.int32, (A, A), 0) == lax.broadcasted_iota(jnp.int32, (A, A), 1)
    energy[...] = jnp.sum(jnp.where(eye, e_col, 0.0), axis=0, keepdims=True)
    t_col = jnp.sum(jnp.where(eye, target[...], 0.0), axis=1, keepdims=True)
    grad_energy = loss_weight * (e_col - t_col)
    slope = sig * (1.0 + updated * (1.0 - sig))
    grad_updated = (grad_energy * readout[...] * slope).astype(bf16)
    grad_att = dot(grad_updated, w_o, NT).astype(bf16)

    def put(m, x):
        grads[2 * m] = x[:, 0:128].astype(bf16)
        grads[2 * m + 1] = x[:, 128:256].astype(bf16)

    put(3, dot(attended, grad_updated, TN))
    g32 = grad_att.astype(f32)
    for h in range(H):
        rep[pl.ds(h, A, stride=8), :] = g32[:, 0:128]
        rep[pl.ds(A * H + h, A, stride=8), :] = g32[:, 128:256]
    gm[...] = spread_heads()
    big[...] = dot(gm[...], v, NT)

    def table_grad(rows_m, mult):
        tg = dot(pt_hi[...], rows_m, NN) + dot(pt_lo[...], rows_m, NN)
        if mult is not None:
            tg = tg * mult
        hi, lo = split(tg)
        return dot(n_all, hi, TN) + dot(n_all, lo, TN)

    put(2, table_grad(gm[...], None))

    @pl.loop(0, 8)
    def _(s):
        r0 = pl.multiple_of(s * 128, 128)
        gw, ok = pick(s)
        a = att[pl.ds(r0, 128), :]
        mean = jnp.sum(a * gw, axis=1, keepdims=True) * 0.5
        scatter(s, (a * (gw - mean)).astype(bf16))

    grad_query = gather_heads(k.astype(f32).T.astype(bf16), scale)
    put(0, dot(n_own, grad_query, TN))
    put(1, table_grad(qm[...], scale))


def attend(emb, nt, wg, nbr, cnt, dist, decay, readout, target):
    vm = pl.BlockSpec(memory_space=pltpu.VMEM)
    sm = pl.BlockSpec(memory_space=pltpu.SMEM)
    return pl.pallas_call(
        attend_kernel,
        out_shape=(
            jax.ShapeDtypeStruct((1, A), f32),
            jax.ShapeDtypeStruct((8, C, 128), bf16),
        ),
        in_specs=[vm] * 6 + [sm] + [vm] * 2,
        out_specs=(vm, vm),
        scratch_shapes=[
            pltpu.VMEM((A * H, 128), jnp.int32),
            pltpu.VMEM((A * H, 128), f32),
            pltpu.VMEM((2 * A * H, 128), f32),
            pltpu.VMEM((A * H, C), bf16),
            pltpu.VMEM((A * H, C), bf16),
            pltpu.VMEM((A * H, T), f32),
            pltpu.VMEM((A * H, 128), f32),
            pltpu.VMEM((128, 1024), bf16),
            pltpu.VMEM((8, T, 1024), bf16),
            pltpu.VMEM((T, A * H), bf16),
            pltpu.VMEM((T, A * H), bf16),
            pltpu.VMEM((A, 128), jnp.int32),
        ],
        name="attend",
    )(emb, nt, wg, nbr, cnt, dist, decay, readout, target)


def reduce_kernel(g, out, r1, s2, r2, fin, sem1, sem2, sem3):
    c = lax.axis_index("cell")
    b = lax.axis_index("brick")
    barrier = pltpu.get_barrier_semaphore()
    for k in range(1, CELLS):
        pl.semaphore_signal(barrier, inc=1, device_id={"cell": lax.rem(c + k, CELLS), "brick": b}, device_id_type=MESH)
    for d in range(1, BRICKS):
        pl.semaphore_signal(barrier, inc=1, device_id={"cell": c, "brick": lax.rem(b + d, BRICKS)}, device_id_type=MESH)
    pl.semaphore_wait(barrier, CELLS - 1 + BRICKS - 1)

    first = []
    for d in range(1, BRICKS):
        to = lax.rem(b + d, BRICKS)
        cp = pltpu.make_async_remote_copy(
            src_ref=g.at[to], dst_ref=r1.at[b], send_sem=sem1.at[0, d], recv_sem=sem1.at[1, d],
            device_id={"cell": c, "brick": to}, device_id_type=MESH)
        cp.start()
        first.append(cp)
    total = g[b].astype(f32)
    for d in range(1, BRICKS):
        first[d - 1].wait_recv()
        total = total + r1[lax.rem(b - d + BRICKS, BRICKS)].astype(f32)
    s2[...] = total.reshape(CELLS, 8, 128).astype(s2.dtype)

    second = []
    for k in range(1, CELLS):
        to = lax.rem(c + k, CELLS)
        cp = pltpu.make_async_remote_copy(
            src_ref=s2.at[to], dst_ref=r2.at[c], send_sem=sem2.at[0, k], recv_sem=sem2.at[1, k],
            device_id={"cell": to, "brick": b}, device_id_type=MESH)
        cp.start()
        second.append(cp)
    r2[c] = s2[c]
    for cp in second:
        cp.wait_recv()
    fin[b] = jnp.sum(r2[...].astype(f32), axis=0)

    third = []
    for d in range(1, BRICKS):
        cp = pltpu.make_async_remote_copy(
            src_ref=fin.at[b], dst_ref=fin.at[b], send_sem=sem3.at[0, d], recv_sem=sem3.at[1, d],
            device_id={"cell": c, "brick": lax.rem(b + d, BRICKS)}, device_id_type=MESH)
        cp.start()
        third.append(cp)
    for cp in first + second:
        cp.wait_send()
    for cp in third:
        cp.wait()
    for m in range(4):
        out[m] = jnp.concatenate([fin[2 * m], fin[2 * m + 1]], axis=1)


def reduce(g):
    vm = pl.BlockSpec(memory_space=pltpu.VMEM)
    return pl.pallas_call(
        reduce_kernel,
        out_shape=jax.ShapeDtypeStruct((4, 8, C), f32),
        in_specs=[vm],
        out_specs=vm,
        scratch_shapes=[
            pltpu.VMEM((BRICKS, C, 128), bf16),
            pltpu.VMEM((CELLS, 8, 128), f32),
            pltpu.VMEM((CELLS, 8, 128), f32),
            pltpu.VMEM((BRICKS, 8, 128), f32),
            pltpu.SemaphoreType.DMA((2, BRICKS)),
            pltpu.SemaphoreType.DMA((2, CELLS)),
            pltpu.SemaphoreType.DMA((2, BRICKS)),
        ],
        compiler_params=pltpu.CompilerParams(collective_id=1, has_side_effects=True),
        name="reduce",
    )(g)


def body(features, species, species_table, neighbours, counts, send_lists, distances,
         head_decay, norm_gain, readout, targets, master, moment, second):
    emb, nt, wg = spread(
        features.reshape(A, C), species.reshape(1, A), species_table,
        send_lists.reshape(BRICKS, 32), norm_gain.reshape(1, C), master)
    energy, grads = attend(
        emb, nt, wg, neighbours.reshape(K, A), counts.reshape(1, A), distances.reshape(K, A),
        head_decay, readout.reshape(1, C), targets.reshape(1, A))
    owned = reduce(grads)
    moment_new = 0.9 * moment + 0.1 * owned
    second_new = 0.999 * second + 0.001 * owned * owned
    adam_step = moment_new / (jnp.sqrt(second_new) + 1e-08)
    return (energy.reshape(1, 1, A), moment_new, second_new, adam_step)


def solution(mesh):
    return jax.shard_map(
        body,
        mesh=mesh,
        in_specs=(
            P("cell", "brick", None, None),
            P("cell", "brick", None),
            P(),
            P("cell", "brick", None, None),
            P("cell", "brick", None),
            P("cell", "brick", None, None),
            P("cell", "brick", None, None),
            P(),
            P(),
            P(),
            P("cell", "brick", None),
            P(None, "cell", None),
            P(None, "cell", None),
            P(None, "cell", None),
        ),
        out_specs=(
            P("cell", "brick", None),
            P(None, "cell", None),
            P(None, "cell", None),
            P(None, "cell", None),
        ),
        check_vma=False,
    )
```

```python
import functools
import math

import jax
import jax.numpy as jnp
from jax import lax
from jax.experimental import pallas as pl
from jax.experimental.pallas import tpu as pltpu
from jax.sharding import PartitionSpec as P

MESH = pl.DeviceIdType.MESH
loss_weight = 0.0625
epsilon_norm = 1e-06
C = 256
H = 8
A = 128
K = 64
T = 384
CELLS = 32
BRICKS = 8
f32 = jnp.float32
bf16 = jnp.bfloat16


def dot(a, b, dims):
    return lax.dot_general(a, b, (dims, ((), ())), preferred_element_type=f32)


NN = ((1,), (0,))
NT = ((1,), (1,))
TN = ((0,), (0,))


def split(x):
    hi = x.astype(bf16)
    return hi, (x - hi.astype(f32)).astype(bf16)


def peer(cell, brick):
    return {"cell": cell, "brick": brick}


def step_kernel(feat, spec, table, sends, gain, master, nbr, cnt, dist, decay, readout, target,
                energy, out,
                emb, nt, wa, wb, parcel,
                idx, dst8, rep, qm, gm, big, att, lmat, onehot, pt_hi, pt_lo, idx2,
                gtmp, gsend, r1, s2f, s2, r2, fin,
                sem_a, sem_b, sem_g, sem_1, sem_2, sem_3):
    c = lax.axis_index("cell")
    b = lax.axis_index("brick")
    partner = c + 1 - 2 * lax.rem(c, 2)
    barrier = pltpu.get_barrier_semaphore()
    for k in range(1, CELLS):
        pl.semaphore_signal(barrier, inc=1, device_id=peer(lax.rem(c + k, CELLS), b), device_id_type=MESH)
    for d in range(1, BRICKS):
        pl.semaphore_signal(barrier, inc=1, device_id=peer(c, lax.rem(b + d, BRICKS)), device_id_type=MESH)

    wa[c] = master[0:2].reshape(16, C).astype(bf16)
    wb[c] = master[2:4].reshape(16, C).astype(bf16)
    eye = lax.broadcasted_iota(jnp.int32, (A, A), 0) == lax.broadcasted_iota(jnp.int32, (A, A), 1)
    col = jnp.sum(jnp.where(eye, jnp.broadcast_to(spec[...], (A, A)), 0).astype(f32), axis=1, keepdims=True)
    e = feat[...].astype(f32)
    tab = table[...].astype(f32)
    add = jnp.zeros((A, C), f32)
    for s in range(4):
        add = jnp.where(col == float(s), tab[s : s + 1, :], add)
    e = e + add
    emb[...] = e
    rms = lax.rsqrt(jnp.sum(e * e, axis=1, keepdims=True) * (1.0 / C) + epsilon_norm)
    n = (e * rms * gain[...]).astype(bf16)
    nt[0:A, :] = n
    row_id = lax.broadcasted_iota(jnp.int32, (A, 32), 0)
    for d in range(BRICKS):
        take = (row_id == sends[d : d + 1, :]).astype(f32).astype(bf16)
        parcel[d] = dot(take, n, TN).astype(bf16)
    nt[pl.ds(pl.multiple_of(A + 32 * b, 32), 32), :] = parcel[b]
    pl.semaphore_wait(barrier, CELLS - 1 + BRICKS - 1)

    def same_core(w, sem):
        made = []
        for k in range(1, 16):
            cp = pltpu.make_async_remote_copy(
                src_ref=w.at[c], dst_ref=w.at[c], send_sem=sem.at[0, k], recv_sem=sem.at[1, k],
                device_id=peer(lax.rem(c + 2 * k, CELLS), b), device_id_type=MESH)
            cp.start()
            made.append(cp)
        return made

    def forward(w, sem, made):
        sent = []
        for k in range(16):
            if k:
                made[k - 1].wait_recv()
            owner = lax.rem(c - 2 * k + CELLS, CELLS)
            cp = pltpu.make_async_remote_copy(
                src_ref=w.at[owner], dst_ref=w.at[owner], send_sem=sem.at[2, k], recv_sem=sem.at[3, k],
                device_id=peer(partner, b), device_id_type=MESH)
            cp.start()
            sent.append(cp)
        return sent

    made_a = same_core(wa, sem_a)
    ghosts = []
    for d in range(1, BRICKS):
        to = lax.rem(b + d, BRICKS)
        cp = pltpu.make_async_remote_copy(
            src_ref=parcel.at[to],
            dst_ref=nt.at[pl.ds(pl.multiple_of(A + 32 * b, 32), 32), :],
            send_sem=sem_g.at[0, d], recv_sem=sem_g.at[1, d],
            device_id=peer(c, to), device_id_type=MESH)
        cp.start()
        ghosts.append(cp)
    made_b = same_core(wb, sem_b)

    scale = 1.0 / math.sqrt(C // H)
    rows = A * H
    slot = lax.broadcasted_iota(jnp.int32, (K, A), 0)
    masked = jnp.where(slot < cnt[...], nbr[...], 512)
    m_t = masked.T
    d_t = dist[...].T
    m2 = jnp.concatenate([m_t, m_t], axis=1)
    d2 = jnp.concatenate([d_t, d_t], axis=1)
    idx2[...] = m2
    for h in range(H):
        idx[pl.ds(h, A, stride=8), :] = m2
        dst8[pl.ds(h, A, stride=8), :] = d2
    lmat[...] = jnp.zeros((128, 1024), bf16)
    t_row = lax.broadcasted_iota(jnp.int32, (T, 128), 0)
    lane8 = lax.broadcasted_iota(jnp.int32, (8, 128), 1)

    @pl.loop(0, 8)
    def _(s):
        ev = idx2[pl.ds(16 * s, 8, stride=2), :]
        od = idx2[pl.ds(16 * s + 1, 8, stride=2), :]
        pair = jnp.where(lane8 < 64, ev, od)
        for t in range(8):
            hit = t_row == pair[t : t + 1, :]
            onehot[s, :, 128 * t : 128 * t + 128] = jnp.where(hit, 1.0, 0.0).astype(bf16)

    sent_a = forward(wa, sem_a, made_a)
    for cp in ghosts:
        cp.wait()
    for cp in sent_a:
        cp.wait_recv()

    def weight(w, m):
        return w[:, 8 * m : 8 * m + 8, :].astype(f32).reshape(C, C).astype(bf16)

    n_all = nt[...]
    n_own = nt[0:A, :]
    q = dot(n_own, weight(wa, 0), NN).astype(bf16)
    k = dot(n_all, weight(wa, 1), NN).astype(bf16)

    head_of_lane = lax.broadcasted_iota(jnp.int32, (rows, C), 1) // 32
    head_of_row = lax.rem(lax.broadcasted_iota(jnp.int32, (rows, C), 0), 8)
    head_mask = head_of_lane == head_of_row

    def spread_heads(x32):
        for h in range(H):
            rep[pl.ds(h, A, stride=8), :] = x32[:, 0:128]
            rep[pl.ds(rows + h, A, stride=8), :] = x32[:, 128:256]
        x = jnp.concatenate([rep[0:rows, :], rep[rows : 2 * rows, :]], axis=1)
        return jnp.where(head_mask, x, 0.0).astype(bf16)

    qm[...] = spread_heads(q.astype(f32))
    big[...] = dot(qm[...], k, NT)
    sent_b = forward(wb, sem_b, made_b)

    lane = lax.broadcasted_iota(jnp.int32, (128, 128), 1)
    row_in = lax.broadcasted_iota(jnp.int32, (128, 128), 0)
    sub_head = lax.rem(row_in, 8)
    dec = jnp.zeros((128, 128), f32)
    for h in range(H):
        dec = jnp.where(sub_head == h, decay[h], dec)
    diag = lax.rem(row_in // 8, 2) == lane // 64

    def pick(s):
        r0 = pl.multiple_of(s * 128, 128)
        ix = idx[pl.ds(r0, 128), :]
        low = jnp.bitwise_and(ix, 127)
        res = jnp.zeros((128, 128), f32)
        for t in range(3):
            g = jnp.take_along_axis(big[pl.ds(r0, 128), 128 * t : 128 * t + 128], low, axis=1)
            res = jnp.where(ix >= 128 * t, g, res)
        return res, ix < 512

    def scatter(s, w32):
        kept = jnp.where(diag, w32, 0.0).astype(bf16)
        for t in range(8):
            lmat[16 * t : 16 * t + 16, 128 * t : 128 * t + 128] = kept[16 * t : 16 * t + 16, :]
        hi, lo = split(dot(onehot[s], lmat[...], NT))
        c0 = pl.multiple_of(s * 128, 128)
        pt_hi[:, pl.ds(c0, 128)] = hi
        pt_lo[:, pl.ds(c0, 128)] = lo

    @pl.loop(0, 8)
    def _(s):
        r0 = pl.multiple_of(s * 128, 128)
        got, ok = pick(s)
        score = got * scale - dec * dst8[pl.ds(r0, 128), :]
        score = jnp.where(ok, score, -1e30)
        top = jnp.max(score, axis=1, keepdims=True)
        ex = jnp.where(ok, jnp.exp(score - top), 0.0)
        a = ex / (jnp.sum(ex, axis=1, keepdims=True) * 0.5)
        att[pl.ds(r0, 128), :] = a
        scatter(s, a)

    for cp in sent_b:
        cp.wait_recv()
    w_o = weight(wb, 1)
    v = dot(n_all, weight(wb, 0), NN).astype(bf16)

    head_sel = (lax.rem(lax.broadcasted_iota(jnp.int32, (C, rows), 1), 8)
                == lax.broadcasted_iota(jnp.int32, (C, rows), 0) // 32)
    collect = (lax.broadcasted_iota(jnp.int32, (A, rows), 1) // 8
               == lax.broadcasted_iota(jnp.int32, (A, rows), 0)).astype(f32).astype(bf16)

    def gather_heads(table_t, mult):
        full = dot(table_t, pt_hi[...], NN) + dot(table_t, pt_lo[...], NN)
        if mult is not None:
            full = full * mult
        kept = jnp.where(head_sel, full, 0.0).astype(bf16)
        return dot(collect, kept, NT).astype(bf16)

    attended = gather_heads(v.astype(f32).T.astype(bf16), None)
    updated = emb[...] + dot(attended, w_o, NN)
    sig = jax.nn.sigmoid(updated)
    e_col = jnp.sum(readout[...] * (updated * sig), axis=1, keepdims=True)
    energy[...] = jnp.sum(jnp.where(eye, e_col, 0.0), axis=0, keepdims=True)
    t_col = jnp.sum(jnp.where(eye, target[...], 0.0), axis=1, keepdims=True)
    grad_energy = loss_weight * (e_col - t_col)
    slope = sig * (1.0 + updated * (1.0 - sig))
    grad_updated = (grad_energy * readout[...] * slope).astype(bf16)
    grad_att = dot(grad_updated, w_o, NT).astype(bf16)

    first = [None] * 4

    def put(m, x):
        gtmp[0:C, :] = x[:, 0:128]
        gtmp[C : 2 * C, :] = x[:, 128:256]
        for d in range(BRICKS):
            gsend[m, d] = jnp.concatenate(
                [gtmp[pl.ds(d, CELLS, stride=8), :], gtmp[pl.ds(C + d, CELLS, stride=8), :]], axis=1).astype(bf16)
        made = []
        for d in range(1, BRICKS):
            to = lax.rem(b + d, BRICKS)
            cp = pltpu.make_async_remote_copy(
                src_ref=gsend.at[m, to], dst_ref=r1.at[m, b], send_sem=sem_1.at[m, 0, d], recv_sem=sem_1.at[m, 1, d],
                device_id=peer(c, to), device_id_type=MESH)
            cp.start()
            made.append(cp)
        first[m] = made

    put(3, dot(attended, grad_updated, TN))
    gm[...] = spread_heads(grad_att.astype(f32))
    big[...] = dot(gm[...], v, NT)

    def table_grad(rows_m, mult):
        tg = dot(pt_hi[...], rows_m, NN) + dot(pt_lo[...], rows_m, NN)
        if mult is not None:
            tg = tg * mult
        hi, lo = split(tg)
        return dot(n_all, hi, TN) + dot(n_all, lo, TN)

    put(2, table_grad(gm[...], None))

    @pl.loop(0, 8)
    def _(s):
        r0 = pl.multiple_of(s * 128, 128)
        gw, ok = pick(s)
        a = att[pl.ds(r0, 128), :]
        mean = jnp.sum(a * gw, axis=1, keepdims=True) * 0.5
        scatter(s, a * (gw - mean))

    put(1, table_grad(qm[...], scale))
    grad_query = gather_heads(k.astype(f32).T.astype(bf16), scale)
    put(0, dot(n_own, grad_query, TN))

    for m in (3, 2, 1, 0):
        total = gsend[m, b].astype(f32)
        for d in range(1, BRICKS):
            first[m][d - 1].wait_recv()
            total = total + r1[m, lax.rem(b - d + BRICKS, BRICKS)].astype(f32)
        s2f[pl.ds(2 * m, CELLS, stride=8), :] = total[:, 0:128]
        s2f[pl.ds(2 * m + 1, CELLS, stride=8), :] = total[:, 128:256]
    s2[...] = s2f[...].reshape(CELLS, 8, 128).astype(bf16)

    second = []
    for k in range(1, CELLS):
        to = lax.rem(c + k, CELLS)
        cp = pltpu.make_async_remote_copy(
            src_ref=s2.at[to], dst_ref=r2.at[c], send_sem=sem_2.at[0, k], recv_sem=sem_2.at[1, k],
            device_id=peer(to, b), device_id_type=MESH)
        cp.start()
        second.append(cp)
    r2[c] = s2[c]
    for cp in made_a + made_b + sent_a + sent_b:
        cp.wait_send()
    for m in range(4):
        for cp in first[m]:
            cp.wait_send()
    for cp in second:
        cp.wait_recv()
    mine = pl.ds(pl.multiple_of(8 * b, 8), 8)
    fin[mine, :] = jnp.sum(r2[...].astype(f32), axis=0)

    third = []
    for d in range(1, BRICKS):
        cp = pltpu.make_async_remote_copy(
            src_ref=fin.at[mine, :], dst_ref=fin.at[mine, :], send_sem=sem_3.at[0, d], recv_sem=sem_3.at[1, d],
            device_id=peer(c, lax.rem(b + d, BRICKS)), device_id_type=MESH)
        cp.start()
        third.append(cp)
    for cp in second:
        cp.wait_send()
    for cp in third:
        cp.wait()
    for m in range(4):
        out[m] = jnp.concatenate([fin[pl.ds(2 * m, 8, stride=8), :], fin[pl.ds(2 * m + 1, 8, stride=8), :]], axis=1)


def step(*args):
    vm = pl.BlockSpec(memory_space=pltpu.VMEM)
    sm = pl.BlockSpec(memory_space=pltpu.SMEM)
    rows = A * H
    dma = pltpu.SemaphoreType.DMA
    return pl.pallas_call(
        step_kernel,
        out_shape=(jax.ShapeDtypeStruct((1, A), f32), jax.ShapeDtypeStruct((4, 8, C), f32)),
        in_specs=[vm] * 9 + [sm] + [vm] * 2,
        out_specs=(vm, vm),
        scratch_shapes=[
            pltpu.VMEM((A, C), f32),
            pltpu.VMEM((T, C), bf16),
            pltpu.VMEM((CELLS, 16, C), bf16),
            pltpu.VMEM((CELLS, 16, C), bf16),
            pltpu.VMEM((BRICKS, 32, C), bf16),
            pltpu.VMEM((rows, 128), jnp.int32),
            pltpu.VMEM((rows, 128), f32),
            pltpu.VMEM((2 * rows, 128), f32),
            pltpu.VMEM((rows, C), bf16),
            pltpu.VMEM((rows, C), bf16),
            pltpu.VMEM((rows, T), f32),
            pltpu.VMEM((rows, 128), f32),
            pltpu.VMEM((128, 1024), bf16),
            pltpu.VMEM((8, T, 1024), bf16),
            pltpu.VMEM((T, rows), bf16),
            pltpu.VMEM((T, rows), bf16),
            pltpu.VMEM((A, 128), jnp.int32),
            pltpu.VMEM((2 * C, 128), f32),
            pltpu.VMEM((4, BRICKS, CELLS, C), bf16),
            pltpu.VMEM((4, BRICKS, CELLS, C), bf16),
            pltpu.VMEM((CELLS * 8, 128), f32),
            pltpu.VMEM((CELLS, 8, 128), bf16),
            pltpu.VMEM((CELLS, 8, 128), bf16),
            pltpu.VMEM((BRICKS * 8, 128), f32),
            dma((4, 16)),
            dma((4, 16)),
            dma((2, BRICKS)),
            dma((4, 2, BRICKS)),
            dma((2, CELLS)),
            dma((2, BRICKS)),
        ],
        compiler_params=pltpu.CompilerParams(collective_id=0, has_side_effects=True),
        name="step",
    )(*args)


def body(features, species, species_table, neighbours, counts, send_lists, distances,
         head_decay, norm_gain, readout, targets, master, moment, second):
    energy, owned = step(
        features.reshape(A, C), species.reshape(1, A), species_table,
        send_lists.reshape(BRICKS, 32), norm_gain.reshape(1, C), master,
        neighbours.reshape(K, A), counts.reshape(1, A), distances.reshape(K, A),
        head_decay, readout.reshape(1, C), targets.reshape(1, A))
    moment_new = 0.9 * moment + 0.1 * owned
    second_new = 0.999 * second + 0.001 * owned * owned
    adam_step = moment_new / (jnp.sqrt(second_new) + 1e-08)
    return (energy.reshape(1, 1, A), moment_new, second_new, adam_step)


def solution(mesh):
    return jax.shard_map(
        body,
        mesh=mesh,
        in_specs=(
            P("cell", "brick", None, None),
            P("cell", "brick", None),
            P(),
            P("cell", "brick", None, None),
            P("cell", "brick", None),
            P("cell", "brick", None, None),
            P("cell", "brick", None, None),
            P(),
            P(),
            P(),
            P("cell", "brick", None),
            P(None, "cell", None),
            P(None, "cell", None),
            P(None, "cell", None),
        ),
        out_specs=(
            P("cell", "brick", None),
            P(None, "cell", None),
            P(None, "cell", None),
            P(None, "cell", None),
        ),
        check_vma=False,
    )
```

```python
import functools
import math

import jax
import jax.numpy as jnp
from jax import lax
from jax.experimental import pallas as pl
from jax.experimental.pallas import tpu as pltpu
from jax.sharding import PartitionSpec as P

MESH = pl.DeviceIdType.MESH
loss_weight = 0.0625
epsilon_norm = 1e-06
C = 256
H = 8
A = 128
K = 64
T = 384
CELLS = 32
BRICKS = 8
f32 = jnp.float32
bf16 = jnp.bfloat16


def dot(a, b, dims):
    return lax.dot_general(a, b, (dims, ((), ())), preferred_element_type=f32)


NN = ((1,), (0,))
NT = ((1,), (1,))
TN = ((0,), (0,))


def split(x):
    hi = x.astype(bf16)
    return hi, (x - hi.astype(f32)).astype(bf16)


def peer(cell, brick):
    return {"cell": cell, "brick": brick}


def step_kernel(master_h, feat_h, spec_h, table_h, gain_h, sends_h, nbr_h, cnt_h, dist_h, decay_h, readout_h, target_h,
                energy, out,
                master, feat, spec, table, gain, sends, nbr, cnt, dist, decay, readout, target, sem_in,
                emb, nt, wa, wb, parcel,
                idx, dst8, rep, qm, gm, big, att, lmat, onehot, pt_hi, pt_lo, idx2,
                n_t, gtmp, gsend, r1, s2f, s2, r2, fin,
                sem_a, sem_b, sem_g, sem_1, sem_2, sem_3):
    c = lax.axis_index("cell")
    b = lax.axis_index("brick")
    partner = c + 1 - 2 * lax.rem(c, 2)
    loads = []
    for i, (src, dst) in enumerate((
            (master_h, master), (feat_h, feat), (spec_h, spec), (table_h, table), (gain_h, gain), (sends_h, sends),
            (nbr_h, nbr), (cnt_h, cnt), (dist_h, dist), (decay_h, decay), (readout_h, readout), (target_h, target))):
        cp = pltpu.make_async_copy(src, dst, sem_in.at[i])
        cp.start()
        loads.append(cp)
    barrier = pltpu.get_barrier_semaphore()
    for k in range(1, CELLS):
        pl.semaphore_signal(barrier, inc=1, device_id=peer(lax.rem(c + k, CELLS), b), device_id_type=MESH)
    for d in range(1, BRICKS):
        pl.semaphore_signal(barrier, inc=1, device_id=peer(c, lax.rem(b + d, BRICKS)), device_id_type=MESH)

    loads[0].wait()
    wa[c] = master[0:2].reshape(16, C).astype(bf16)
    wb[c] = master[2:4].reshape(16, C).astype(bf16)
    pl.semaphore_wait(barrier, CELLS - 1 + BRICKS - 1)

    def same_core(w, sem):
        made = []
        for k in range(1, 16):
            cp = pltpu.make_async_remote_copy(
                src_ref=w.at[c], dst_ref=w.at[c], send_sem=sem.at[0, k], recv_sem=sem.at[1, k],
                device_id=peer(lax.rem(c + 2 * k, CELLS), b), device_id_type=MESH)
            cp.start()
            made.append(cp)
        return made

    def forward(w, sem, made):
        sent = []
        for k in range(16):
            if k:
                made[k - 1].wait_recv()
            owner = lax.rem(c - 2 * k + CELLS, CELLS)
            cp = pltpu.make_async_remote_copy(
                src_ref=w.at[owner], dst_ref=w.at[owner], send_sem=sem.at[2, k], recv_sem=sem.at[3, k],
                device_id=peer(partner, b), device_id_type=MESH)
            cp.start()
            sent.append(cp)
        return sent

    made_a = same_core(wa, sem_a)
    for cp in loads[1:6]:
        cp.wait()
    eye = lax.broadcasted_iota(jnp.int32, (A, A), 0) == lax.broadcasted_iota(jnp.int32, (A, A), 1)
    col = jnp.sum(jnp.where(eye, jnp.broadcast_to(spec[...], (A, A)), 0).astype(f32), axis=1, keepdims=True)
    e = feat[...].astype(f32)
    tab = table[...].astype(f32)
    add = jnp.zeros((A, C), f32)
    for s in range(4):
        add = jnp.where(col == float(s), tab[s : s + 1, :], add)
    e = e + add
    emb[...] = e
    rms = lax.rsqrt(jnp.sum(e * e, axis=1, keepdims=True) * (1.0 / C) + epsilon_norm)
    n = (e * rms * gain[...]).astype(bf16)
    nt[0:A, :] = n
    row_id = lax.broadcasted_iota(jnp.int32, (A, 32), 0)
    for d in range(BRICKS):
        take = (row_id == sends[d : d + 1, :]).astype(f32).astype(bf16)
        parcel[d] = dot(take, n, TN).astype(bf16)
    nt[pl.ds(pl.multiple_of(A + 32 * b, 32), 32), :] = parcel[b]
    ghosts = []
    for d in range(1, BRICKS):
        to = lax.rem(b + d, BRICKS)
        cp = pltpu.make_async_remote_copy(
            src_ref=parcel.at[to],
            dst_ref=nt.at[pl.ds(pl.multiple_of(A + 32 * b, 32), 32), :],
            send_sem=sem_g.at[0, d], recv_sem=sem_g.at[1, d],
            device_id=peer(c, to), device_id_type=MESH)
        cp.start()
        ghosts.append(cp)
    made_b = same_core(wb, sem_b)
    for cp in loads[6:]:
        cp.wait()

    scale = 1.0 / math.sqrt(C // H)
    rows = A * H
    slot = lax.broadcasted_iota(jnp.int32, (K, A), 0)
    masked = jnp.where(slot < cnt[...], nbr[...], 512)
    m_t = masked.T
    d_t = dist[...].T
    m2 = jnp.concatenate([m_t, m_t], axis=1)
    d2 = jnp.concatenate([d_t, d_t], axis=1)
    idx2[...] = m2
    for h in range(H):
        idx[pl.ds(h, A, stride=8), :] = m2
        dst8[pl.ds(h, A, stride=8), :] = d2
    lmat[...] = jnp.zeros((8, 128, 1024), bf16)
    t_row = lax.broadcasted_iota(jnp.int32, (T, 128), 0)
    lane8 = lax.broadcasted_iota(jnp.int32, (8, 128), 1)

    @pl.loop(0, 8)
    def _(s):
        ev = idx2[pl.ds(16 * s, 8, stride=2), :]
        od = idx2[pl.ds(16 * s + 1, 8, stride=2), :]
        pair = jnp.where(lane8 < 64, ev, od)
        for t in range(8):
            hit = t_row == pair[t : t + 1, :]
            onehot[s, :, 128 * t : 128 * t + 128] = jnp.where(hit, 1.0, 0.0).astype(bf16)

    for cp in ghosts:
        cp.wait()
    n_t[...] = nt[...].astype(f32).T.astype(bf16)
    sent_a = forward(wa, sem_a, made_a)
    for cp in sent_a:
        cp.wait_recv()

    def weight(w, m):
        return w[:, 8 * m : 8 * m + 8, :].astype(f32).reshape(C, C).astype(bf16)

    n_all = nt[...]
    n_own = nt[0:A, :]
    q = dot(n_own, weight(wa, 0), NN).astype(bf16)
    k = dot(n_all, weight(wa, 1), NN).astype(bf16)

    head_of_lane = lax.broadcasted_iota(jnp.int32, (rows, C), 1) // 32
    head_of_row = lax.rem(lax.broadcasted_iota(jnp.int32, (rows, C), 0), 8)
    head_mask = head_of_lane == head_of_row

    def spread_heads(x32):
        for h in range(H):
            rep[pl.ds(h, A, stride=8), :] = x32[:, 0:128]
            rep[pl.ds(rows + h, A, stride=8), :] = x32[:, 128:256]
        x = jnp.concatenate([rep[0:rows, :], rep[rows : 2 * rows, :]], axis=1)
        return jnp.where(head_mask, x, 0.0).astype(bf16)

    qm[...] = spread_heads(q.astype(f32))
    big[...] = dot(qm[...], k, NT)
    sent_b = forward(wb, sem_b, made_b)

    lane = lax.broadcasted_iota(jnp.int32, (128, 128), 1)
    row_in = lax.broadcasted_iota(jnp.int32, (128, 128), 0)
    sub_head = lax.rem(row_in, 8)
    dec = jnp.zeros((128, 128), f32)
    for h in range(H):
        dec = jnp.where(sub_head == h, decay[:, h : h + 1], dec)
    diag = lax.rem(row_in // 8, 2) == lane // 64

    def pick(s):
        r0 = s * 128
        ix = idx[pl.ds(r0, 128), :]
        low = jnp.bitwise_and(ix, 127)
        res = jnp.zeros((128, 128), f32)
        for t in range(3):
            g = jnp.take_along_axis(big[pl.ds(r0, 128), 128 * t : 128 * t + 128], low, axis=1)
            res = jnp.where(ix >= 128 * t, g, res)
        return res, ix < 512

    def scatter(s, w32):
        kept = jnp.where(diag, w32, 0.0).astype(bf16)
        for t in range(8):
            lmat[s, 16 * t : 16 * t + 16, 128 * t : 128 * t + 128] = kept[16 * t : 16 * t + 16, :]

    def collect_rows(s):
        hi, lo = split(dot(onehot[s], lmat[s], NT))
        pt_hi[:, 128 * s : 128 * s + 128] = hi
        pt_lo[:, 128 * s : 128 * s + 128] = lo

    for s in range(8):
        r0 = s * 128
        got, ok = pick(s)
        score = got * scale - dec * dst8[pl.ds(r0, 128), :]
        score = jnp.where(ok, score, -1e30)
        top = jnp.max(score, axis=1, keepdims=True)
        ex = jnp.where(ok, jnp.exp(score - top), 0.0)
        a = ex / (jnp.sum(ex, axis=1, keepdims=True) * 0.5)
        att[pl.ds(r0, 128), :] = a
        scatter(s, a)
        if s:
            collect_rows(s - 1)
    collect_rows(7)

    for cp in sent_b:
        cp.wait_recv()
    w_o = weight(wb, 1)
    v = dot(n_all, weight(wb, 0), NN).astype(bf16)

    head_sel = (lax.rem(lax.broadcasted_iota(jnp.int32, (C, rows), 1), 8)
                == lax.broadcasted_iota(jnp.int32, (C, rows), 0) // 32)
    collect = (lax.broadcasted_iota(jnp.int32, (A, rows), 1) // 8
               == lax.broadcasted_iota(jnp.int32, (A, rows), 0)).astype(f32).astype(bf16)

    def gather_heads(table_t, mult):
        full = dot(table_t, pt_hi[...], NN) + dot(table_t, pt_lo[...], NN)
        if mult is not None:
            full = full * mult
        kept = jnp.where(head_sel, full, 0.0).astype(bf16)
        return dot(collect, kept, NT).astype(bf16)

    attended = gather_heads(v.astype(f32).T.astype(bf16), None)
    updated = emb[...] + dot(attended, w_o, NN)
    sig = jax.nn.sigmoid(updated)
    e_col = jnp.sum(readout[...] * (updated * sig), axis=1, keepdims=True)
    energy[...] = jnp.sum(jnp.where(eye, e_col, 0.0), axis=0, keepdims=True)
    t_col = jnp.sum(jnp.where(eye, target[...], 0.0), axis=1, keepdims=True)
    grad_energy = loss_weight * (e_col - t_col)
    slope = sig * (1.0 + updated * (1.0 - sig))
    grad_updated = (grad_energy * readout[...] * slope).astype(bf16)
    grad_att = dot(grad_updated, w_o, NT).astype(bf16)

    first = [None] * 4

    def put(m, x):
        gtmp[0:C, :] = x[:, 0:128]
        gtmp[C : 2 * C, :] = x[:, 128:256]
        for d in range(BRICKS):
            gsend[m, d] = jnp.concatenate(
                [gtmp[pl.ds(d, CELLS, stride=8), :], gtmp[pl.ds(C + d, CELLS, stride=8), :]], axis=1).astype(bf16)
        made = []
        for d in range(1, BRICKS):
            to = lax.rem(b + d, BRICKS)
            cp = pltpu.make_async_remote_copy(
                src_ref=gsend.at[m, to], dst_ref=r1.at[m, b], send_sem=sem_1.at[m, 0, d], recv_sem=sem_1.at[m, 1, d],
                device_id=peer(c, to), device_id_type=MESH)
            cp.start()
            made.append(cp)
        first[m] = made

    put(3, dot(attended, grad_updated, TN))
    gm[...] = spread_heads(grad_att.astype(f32))
    big[...] = dot(gm[...], v, NT)

    def table_grad(rows_m, mult):
        tg = dot(pt_hi[...], rows_m, NN) + dot(pt_lo[...], rows_m, NN)
        if mult is not None:
            tg = tg * mult
        hi, lo = split(tg)
        return dot(n_t[...], hi, NN) + dot(n_t[...], lo, NN)

    put(2, table_grad(gm[...], None))

    for s in range(8):
        r0 = s * 128
        gw, ok = pick(s)
        a = att[pl.ds(r0, 128), :]
        mean = jnp.sum(a * gw, axis=1, keepdims=True) * 0.5
        scatter(s, a * (gw - mean))
        if s:
            collect_rows(s - 1)
    collect_rows(7)

    put(1, table_grad(qm[...], scale))
    grad_query = gather_heads(k.astype(f32).T.astype(bf16), scale)
    put(0, dot(n_t[:, 0:A], grad_query, NN))

    for m in (3, 2, 1, 0):
        total = gsend[m, b].astype(f32)
        for d in range(1, BRICKS):
            first[m][d - 1].wait_recv()
            total = total + r1[m, lax.rem(b - d + BRICKS, BRICKS)].astype(f32)
        s2f[pl.ds(2 * m, CELLS, stride=8), :] = total[:, 0:128]
        s2f[pl.ds(2 * m + 1, CELLS, stride=8), :] = total[:, 128:256]
    s2[...] = s2f[...].reshape(CELLS, 8, 128).astype(bf16)

    second = []
    for k in range(1, CELLS):
        to = lax.rem(c + k, CELLS)
        cp = pltpu.make_async_remote_copy(
            src_ref=s2.at[to], dst_ref=r2.at[c], send_sem=sem_2.at[0, k], recv_sem=sem_2.at[1, k],
            device_id=peer(to, b), device_id_type=MESH)
        cp.start()
        second.append(cp)
    r2[c] = s2[c]
    for cp in made_a + made_b + sent_a + sent_b:
        cp.wait_send()
    for m in range(4):
        for cp in first[m]:
            cp.wait_send()
    for cp in second:
        cp.wait_recv()
    mine = pl.ds(pl.multiple_of(8 * b, 8), 8)
    fin[mine, :] = jnp.sum(r2[...].astype(f32), axis=0)

    third = []
    for d in range(1, BRICKS):
        cp = pltpu.make_async_remote_copy(
            src_ref=fin.at[mine, :], dst_ref=fin.at[mine, :], send_sem=sem_3.at[0, d], recv_sem=sem_3.at[1, d],
            device_id=peer(c, lax.rem(b + d, BRICKS)), device_id_type=MESH)
        cp.start()
        third.append(cp)
    for cp in second:
        cp.wait_send()
    for cp in third:
        cp.wait()
    for m in range(4):
        out[m] = jnp.concatenate([fin[pl.ds(2 * m, 8, stride=8), :], fin[pl.ds(2 * m + 1, 8, stride=8), :]], axis=1)


def step(*args):
    vm = pl.BlockSpec(memory_space=pltpu.VMEM)
    rows = A * H
    dma = pltpu.SemaphoreType.DMA
    return pl.pallas_call(
        step_kernel,
        out_shape=(jax.ShapeDtypeStruct((1, A), f32), jax.ShapeDtypeStruct((4, 8, C), f32)),
        in_specs=[pl.BlockSpec(memory_space=pl.ANY)] * 12,
        out_specs=(vm, vm),
        scratch_shapes=[
            pltpu.VMEM((4, 8, C), f32),
            pltpu.VMEM((A, C), bf16),
            pltpu.VMEM((1, A), jnp.int32),
            pltpu.VMEM((4, C), bf16),
            pltpu.VMEM((1, C), f32),
            pltpu.VMEM((BRICKS, 32), jnp.int32),
            pltpu.VMEM((K, A), jnp.int32),
            pltpu.VMEM((1, A), jnp.int32),
            pltpu.VMEM((K, A), f32),
            pltpu.VMEM((1, H), f32),
            pltpu.VMEM((1, C), f32),
            pltpu.VMEM((1, A), f32),
            dma((12,)),
            pltpu.VMEM((A, C), f32),
            pltpu.VMEM((T, C), bf16),
            pltpu.VMEM((CELLS, 16, C), bf16),
            pltpu.VMEM((CELLS, 16, C), bf16),
            pltpu.VMEM((BRICKS, 32, C), bf16),
            pltpu.VMEM((rows, 128), jnp.int32),
            pltpu.VMEM((rows, 128), f32),
            pltpu.VMEM((2 * rows, 128), f32),
            pltpu.VMEM((rows, C), bf16),
            pltpu.VMEM((rows, C), bf16),
            pltpu.VMEM((rows, T), f32),
            pltpu.VMEM((rows, 128), f32),
            pltpu.VMEM((8, 128, 1024), bf16),
            pltpu.VMEM((8, T, 1024), bf16),
            pltpu.VMEM((T, rows), bf16),
            pltpu.VMEM((T, rows), bf16),
            pltpu.VMEM((A, 128), jnp.int32),
            pltpu.VMEM((C, T), bf16),
            pltpu.VMEM((2 * C, 128), f32),
            pltpu.VMEM((4, BRICKS, CELLS, C), bf16),
            pltpu.VMEM((4, BRICKS, CELLS, C), bf16),
            pltpu.VMEM((CELLS * 8, 128), f32),
            pltpu.VMEM((CELLS, 8, 128), bf16),
            pltpu.VMEM((CELLS, 8, 128), bf16),
            pltpu.VMEM((BRICKS * 8, 128), f32),
            dma((4, 16)),
            dma((4, 16)),
            dma((2, BRICKS)),
            dma((4, 2, BRICKS)),
            dma((2, CELLS)),
            dma((2, BRICKS)),
        ],
        compiler_params=pltpu.CompilerParams(collective_id=0, has_side_effects=True),
        name="step",
    )(*args)


def update_kernel(energy, owned, moment, second, energy_out, moment_out, second_out, step_out):
    g = owned[...]
    m = 0.9 * moment[...] + 0.1 * g
    s = 0.999 * second[...] + 0.001 * g * g
    moment_out[...] = m
    second_out[...] = s
    step_out[...] = m / (jnp.sqrt(s) + 1e-08)
    energy_out[...] = energy[...]


def update(energy, owned, moment, second):
    vm = pl.BlockSpec(memory_space=pltpu.VMEM)
    block = jax.ShapeDtypeStruct((4, 8, C), f32)
    return pl.pallas_call(
        update_kernel,
        out_shape=(jax.ShapeDtypeStruct((1, A), f32), block, block, block),
        in_specs=[vm] * 4,
        out_specs=(vm,) * 4,
        name="update",
    )(energy, owned, moment, second)


def body(features, species, species_table, neighbours, counts, send_lists, distances,
         head_decay, norm_gain, readout, targets, master, moment, second):
    energy, owned = step(
        master, features.reshape(A, C), species.reshape(1, A), species_table,
        norm_gain.reshape(1, C), send_lists.reshape(BRICKS, 32),
        neighbours.reshape(K, A), counts.reshape(1, A), distances.reshape(K, A),
        head_decay.reshape(1, H), readout.reshape(1, C), targets.reshape(1, A))
    energies, moment_new, second_new, adam_step = update(energy, owned, moment, second)
    return (energies.reshape(1, 1, A), moment_new, second_new, adam_step)


def solution(mesh):
    return jax.shard_map(
        body,
        mesh=mesh,
        in_specs=(
            P("cell", "brick", None, None),
            P("cell", "brick", None),
            P(),
            P("cell", "brick", None, None),
            P("cell", "brick", None),
            P("cell", "brick", None, None),
            P("cell", "brick", None, None),
            P(),
            P(),
            P(),
            P("cell", "brick", None),
            P(None, "cell", None),
            P(None, "cell", None),
            P(None, "cell", None),
        ),
        out_specs=(
            P("cell", "brick", None),
            P(None, "cell", None),
            P(None, "cell", None),
            P(None, "cell", None),
        ),
        check_vma=False,
    )
```

```python
import functools
import math

import jax
import jax.numpy as jnp
from jax import lax
from jax.experimental import pallas as pl
from jax.experimental.pallas import tpu as pltpu
from jax.sharding import PartitionSpec as P

MESH = pl.DeviceIdType.MESH
loss_weight = 0.0625
epsilon_norm = 1e-06
C = 256
H = 8
A = 128
K = 64
T = 384
CELLS = 32
BRICKS = 8
f32 = jnp.float32
bf16 = jnp.bfloat16


def dot(a, b, dims):
    return lax.dot_general(a, b, (dims, ((), ())), preferred_element_type=f32)


NN = ((1,), (0,))
NT = ((1,), (1,))
TN = ((0,), (0,))


def split(x):
    hi = x.astype(bf16)
    return hi, (x - hi.astype(f32)).astype(bf16)


def peer(cell, brick):
    return {"cell": cell, "brick": brick}


def step_kernel(master_h, feat_h, spec_h, table_h, gain_h, sends_h, nbr_h, cnt_h, dist_h, decay_h, readout_h, target_h,
                energy, out,
                master, feat, spec, table, gain, sends, nbr, cnt, dist, decay, readout, target, sem_in,
                emb, nt, wa, wb, parcel,
                idx, dst8, rep, qm, gm, big, att, lmat, onehot, pt_hi, pt_lo, idx2,
                n_t, gtmp, gsend, r1, s2f, s2, r2, fin,
                sem_a, sem_b, sem_g, sem_1, sem_2, sem_3):
    c = lax.axis_index("cell")
    b = lax.axis_index("brick")
    partner = c + 1 - 2 * lax.rem(c, 2)
    loads = []
    for i, (src, dst) in enumerate((
            (master_h, master), (feat_h, feat), (spec_h, spec), (table_h, table), (gain_h, gain), (sends_h, sends),
            (nbr_h, nbr), (cnt_h, cnt), (dist_h, dist), (decay_h, decay), (readout_h, readout), (target_h, target))):
        cp = pltpu.make_async_copy(src, dst, sem_in.at[i])
        cp.start()
        loads.append(cp)
    barrier = pltpu.get_barrier_semaphore()
    low = lax.rem(c, 16)
    base = c - low
    other = 16 - base

    def at(dz, flip):
        return lax.rem(low + 2 * dz + 16, 16) + (other if flip else base)

    def column(flip):
        return b + 1 - 2 * lax.rem(b, 2) if flip else b

    spots = [(1, 0), (1, 1), (2, 0), (2, 1), (-1, 0), (-1, 1), (-2, 0), (-2, 1), (0, 1)]
    hops = [(2, -1, 0), (2, -1, 1), (2, -2, 0), (2, -2, 1), (-2, 1, 0), (-2, 1, 1)]

    def plane(i):
        return peer(at(0, i // 8), lax.rem(b + i % 8, BRICKS))

    for i in range(1, 16):
        pl.semaphore_signal(barrier, inc=1, device_id=plane(i), device_id_type=MESH)
    for dz, flip in spots[:8]:
        pl.semaphore_signal(barrier, inc=1, device_id=peer(at(dz, flip), column(flip)), device_id_type=MESH)
    pl.semaphore_signal(barrier, inc=1, device_id=peer(partner, b), device_id_type=MESH)
    loads[0].wait()
    wa[c] = master[0:2].reshape(16, C).astype(bf16)
    wb[c] = master[2:4].reshape(16, C).astype(bf16)
    pl.semaphore_wait(barrier, 24)

    def send(w, sem, half, i, block, cell, brick):
        cp = pltpu.make_async_remote_copy(
            src_ref=w.at[block], dst_ref=w.at[block], send_sem=sem.at[half, i], recv_sem=sem.at[half + 1, i],
            device_id=peer(cell, brick), device_id_type=MESH)
        cp.start()
        return cp

    def share(w, sem, i, block):
        return send(w, sem, 2, i, block, partner, b)

    def start_near(w, sem):
        near = [send(w, sem, 0, i, c, at(dz, flip), column(flip)) for i, (dz, flip) in enumerate(spots)]
        return near, [share(w, sem, 15, c)]

    def relay(w, sem, near, shared):
        far = []
        for i, (dz, flip) in enumerate(spots):
            near[i].wait_recv()
            block = at(-dz, flip)
            for j, (to, off, kind) in enumerate(hops):
                if (-dz, flip) == (off, kind):
                    far.append(send(w, sem, 0, 9 + j, block, at(to, 0), b))
            shared.append(share(w, sem, i, block))
        return far

    def finish(w, sem, far, shared):
        for j, (to, off, kind) in enumerate(hops):
            far[j].wait_recv()
            shared.append(share(w, sem, 9 + j, at(off - to, kind)))

    near_a, shared_a = start_near(wa, sem_a)
    for cp in loads[1:6]:
        cp.wait()
    eye = lax.broadcasted_iota(jnp.int32, (A, A), 0) == lax.broadcasted_iota(jnp.int32, (A, A), 1)
    col = jnp.sum(jnp.where(eye, jnp.broadcast_to(spec[...], (A, A)), 0).astype(f32), axis=1, keepdims=True)
    e = feat[...].astype(f32)
    tab = table[...].astype(f32)
    add = jnp.zeros((A, C), f32)
    for s in range(4):
        add = jnp.where(col == float(s), tab[s : s + 1, :], add)
    e = e + add
    emb[...] = e
    rms = lax.rsqrt(jnp.sum(e * e, axis=1, keepdims=True) * (1.0 / C) + epsilon_norm)
    n = (e * rms * gain[...]).astype(bf16)
    nt[0:A, :] = n
    row_id = lax.broadcasted_iota(jnp.int32, (A, 32), 0)
    for d in range(BRICKS):
        take = (row_id == sends[d : d + 1, :]).astype(f32).astype(bf16)
        parcel[d] = dot(take, n, TN).astype(bf16)
    nt[pl.ds(pl.multiple_of(A + 32 * b, 32), 32), :] = parcel[b]
    ghosts = []
    for d in range(1, BRICKS):
        to = lax.rem(b + d, BRICKS)
        cp = pltpu.make_async_remote_copy(
            src_ref=parcel.at[to],
            dst_ref=nt.at[pl.ds(pl.multiple_of(A + 32 * b, 32), 32), :],
            send_sem=sem_g.at[0, d], recv_sem=sem_g.at[1, d],
            device_id=peer(c, to), device_id_type=MESH)
        cp.start()
        ghosts.append(cp)
    near_b, shared_b = start_near(wb, sem_b)
    for cp in loads[6:]:
        cp.wait()

    scale = 1.0 / math.sqrt(C // H)
    rows = A * H
    slot = lax.broadcasted_iota(jnp.int32, (K, A), 0)
    masked = jnp.where(slot < cnt[...], nbr[...], 512)
    m_t = masked.T
    d_t = dist[...].T
    m2 = jnp.concatenate([m_t, m_t], axis=1)
    d2 = jnp.concatenate([d_t, d_t], axis=1)
    idx2[...] = m2
    for h in range(H):
        idx[pl.ds(h, A, stride=8), :] = m2
        dst8[pl.ds(h, A, stride=8), :] = d2
    lmat[...] = jnp.zeros((8, 128, 1024), bf16)
    far_a = relay(wa, sem_a, near_a, shared_a)
    far_b = relay(wb, sem_b, near_b, shared_b)
    t_row = lax.broadcasted_iota(jnp.int32, (T, 128), 0)
    lane8 = lax.broadcasted_iota(jnp.int32, (8, 128), 1)

    @pl.loop(0, 8)
    def _(s):
        ev = idx2[pl.ds(16 * s, 8, stride=2), :]
        od = idx2[pl.ds(16 * s + 1, 8, stride=2), :]
        pair = jnp.where(lane8 < 64, ev, od)
        for t in range(8):
            hit = t_row == pair[t : t + 1, :]
            onehot[s, :, 128 * t : 128 * t + 128] = jnp.where(hit, 1.0, 0.0).astype(bf16)

    finish(wa, sem_a, far_a, shared_a)
    for cp in ghosts:
        cp.wait()
    n_t[...] = nt[...].astype(f32).T.astype(bf16)
    for cp in shared_a:
        cp.wait_recv()

    def weight(w, m):
        return w[:, 8 * m : 8 * m + 8, :].astype(f32).reshape(C, C).astype(bf16)

    n_all = nt[...]
    n_own = nt[0:A, :]
    q = dot(n_own, weight(wa, 0), NN).astype(bf16)
    k = dot(n_all, weight(wa, 1), NN).astype(bf16)

    head_of_lane = lax.broadcasted_iota(jnp.int32, (rows, C), 1) // 32
    head_of_row = lax.rem(lax.broadcasted_iota(jnp.int32, (rows, C), 0), 8)
    head_mask = head_of_lane == head_of_row

    def spread_heads(x32):
        for h in range(H):
            rep[pl.ds(h, A, stride=8), :] = x32[:, 0:128]
            rep[pl.ds(rows + h, A, stride=8), :] = x32[:, 128:256]
        x = jnp.concatenate([rep[0:rows, :], rep[rows : 2 * rows, :]], axis=1)
        return jnp.where(head_mask, x, 0.0).astype(bf16)

    qm[...] = spread_heads(q.astype(f32))
    big[...] = dot(qm[...], k, NT)
    finish(wb, sem_b, far_b, shared_b)

    lane = lax.broadcasted_iota(jnp.int32, (128, 128), 1)
    row_in = lax.broadcasted_iota(jnp.int32, (128, 128), 0)
    sub_head = lax.rem(row_in, 8)
    dec = jnp.zeros((128, 128), f32)
    for h in range(H):
        dec = jnp.where(sub_head == h, decay[:, h : h + 1], dec)
    diag = lax.rem(row_in // 8, 2) == lane // 64

    def pick(s):
        r0 = s * 128
        ix = idx[pl.ds(r0, 128), :]
        low = jnp.bitwise_and(ix, 127)
        res = jnp.zeros((128, 128), f32)
        for t in range(3):
            g = jnp.take_along_axis(big[pl.ds(r0, 128), 128 * t : 128 * t + 128], low, axis=1)
            res = jnp.where(ix >= 128 * t, g, res)
        return res, ix < 512

    def scatter(s, w32):
        kept = jnp.where(diag, w32, 0.0).astype(bf16)
        for t in range(8):
            lmat[s, 16 * t : 16 * t + 16, 128 * t : 128 * t + 128] = kept[16 * t : 16 * t + 16, :]

    def collect_rows(s):
        hi, lo = split(dot(onehot[s], lmat[s], NT))
        pt_hi[:, 128 * s : 128 * s + 128] = hi
        pt_lo[:, 128 * s : 128 * s + 128] = lo

    for s in range(8):
        r0 = s * 128
        got, ok = pick(s)
        score = got * scale - dec * dst8[pl.ds(r0, 128), :]
        score = jnp.where(ok, score, -1e30)
        top = jnp.max(score, axis=1, keepdims=True)
        ex = jnp.where(ok, jnp.exp(score - top), 0.0)
        a = ex / (jnp.sum(ex, axis=1, keepdims=True) * 0.5)
        att[pl.ds(r0, 128), :] = a
        scatter(s, a)
        if s:
            collect_rows(s - 1)
    collect_rows(7)

    for cp in shared_b:
        cp.wait_recv()
    w_o = weight(wb, 1)
    v = dot(n_all, weight(wb, 0), NN).astype(bf16)

    head_sel = (lax.rem(lax.broadcasted_iota(jnp.int32, (C, rows), 1), 8)
                == lax.broadcasted_iota(jnp.int32, (C, rows), 0) // 32)
    collect = (lax.broadcasted_iota(jnp.int32, (A, rows), 1) // 8
               == lax.broadcasted_iota(jnp.int32, (A, rows), 0)).astype(f32).astype(bf16)

    def gather_heads(table_t, mult):
        full = dot(table_t, pt_hi[...], NN) + dot(table_t, pt_lo[...], NN)
        if mult is not None:
            full = full * mult
        kept = jnp.where(head_sel, full, 0.0).astype(bf16)
        return dot(collect, kept, NT).astype(bf16)

    attended = gather_heads(v.astype(f32).T.astype(bf16), None)
    updated = emb[...] + dot(attended, w_o, NN)
    sig = jax.nn.sigmoid(updated)
    e_col = jnp.sum(readout[...] * (updated * sig), axis=1, keepdims=True)
    energy[...] = jnp.sum(jnp.where(eye, e_col, 0.0), axis=0, keepdims=True)
    t_col = jnp.sum(jnp.where(eye, target[...], 0.0), axis=1, keepdims=True)
    grad_energy = loss_weight * (e_col - t_col)
    slope = sig * (1.0 + updated * (1.0 - sig))
    grad_updated = (grad_energy * readout[...] * slope).astype(bf16)
    grad_att = dot(grad_updated, w_o, NT).astype(bf16)

    first = [None] * 4

    def put(m, x):
        gtmp[0:C, :] = x[:, 0:128]
        gtmp[C : 2 * C, :] = x[:, 128:256]
        for d in range(BRICKS):
            gsend[m, d] = jnp.concatenate(
                [gtmp[pl.ds(d, CELLS, stride=8), :], gtmp[pl.ds(C + d, CELLS, stride=8), :]], axis=1).astype(bf16)
        made = []
        for i in range(1, 16):
            half = pl.ds(pl.multiple_of(other if i // 8 else base, 16), 16)
            cp = pltpu.make_async_remote_copy(
                src_ref=gsend.at[m, lax.rem(b + i % 8, BRICKS), half, :], dst_ref=r1.at[m, base // 2 + b],
                send_sem=sem_1.at[m, 0, i], recv_sem=sem_1.at[m, 1, i],
                device_id=plane(i), device_id_type=MESH)
            cp.start()
            made.append(cp)
        first[m] = made

    put(3, dot(attended, grad_updated, TN))
    gm[...] = spread_heads(grad_att.astype(f32))
    big[...] = dot(gm[...], v, NT)

    def table_grad(rows_m, mult):
        tg = dot(pt_hi[...], rows_m, NN) + dot(pt_lo[...], rows_m, NN)
        if mult is not None:
            tg = tg * mult
        hi, lo = split(tg)
        return dot(n_t[...], hi, NN) + dot(n_t[...], lo, NN)

    put(2, table_grad(gm[...], None))

    for s in range(8):
        r0 = s * 128
        gw, ok = pick(s)
        a = att[pl.ds(r0, 128), :]
        mean = jnp.sum(a * gw, axis=1, keepdims=True) * 0.5
        scatter(s, a * (gw - mean))
        if s:
            collect_rows(s - 1)
    collect_rows(7)

    put(1, table_grad(qm[...], scale))
    grad_query = gather_heads(k.astype(f32).T.astype(bf16), scale)
    put(0, dot(n_t[:, 0:A], grad_query, NN))

    for m in (3, 2, 1, 0):
        total = gsend[m, b, pl.ds(pl.multiple_of(base, 16), 16), :].astype(f32)
        for i in range(1, 16):
            first[m][i - 1].wait_recv()
            source = (other if i // 8 else base) // 2 + lax.rem(b - i % 8 + BRICKS, BRICKS)
            total = total + r1[m, source].astype(f32)
        s2f[pl.ds(2 * m, 16, stride=8), :] = total[:, 0:128]
        s2f[pl.ds(2 * m + 1, 16, stride=8), :] = total[:, 128:256]
    s2[...] = s2f[...].reshape(16, 8, 128).astype(bf16)

    second = []
    for k in range(1, 16):
        to = lax.rem(low + k, 16)
        cp = pltpu.make_async_remote_copy(
            src_ref=s2.at[to], dst_ref=r2.at[low], send_sem=sem_2.at[0, k], recv_sem=sem_2.at[1, k],
            device_id=peer(base + to, b), device_id_type=MESH)
        cp.start()
        second.append(cp)
    r2[low] = s2[low]
    for cp in near_a + near_b + far_a + far_b + shared_a + shared_b:
        cp.wait_send()
    for m in range(4):
        for cp in first[m]:
            cp.wait_send()
    for cp in second:
        cp.wait_recv()
    mine = pl.ds(pl.multiple_of(8 * b, 8), 8)
    fin[mine, :] = jnp.sum(r2[...].astype(f32), axis=0)

    third = []
    for d in range(1, BRICKS):
        cp = pltpu.make_async_remote_copy(
            src_ref=fin.at[mine, :], dst_ref=fin.at[mine, :], send_sem=sem_3.at[0, d], recv_sem=sem_3.at[1, d],
            device_id=peer(c, lax.rem(b + d, BRICKS)), device_id_type=MESH)
        cp.start()
        third.append(cp)
    for cp in second:
        cp.wait_send()
    for cp in third:
        cp.wait()
    for m in range(4):
        out[m] = jnp.concatenate([fin[pl.ds(2 * m, 8, stride=8), :], fin[pl.ds(2 * m + 1, 8, stride=8), :]], axis=1)


def step(*args):
    vm = pl.BlockSpec(memory_space=pltpu.VMEM)
    rows = A * H
    dma = pltpu.SemaphoreType.DMA
    return pl.pallas_call(
        step_kernel,
        out_shape=(jax.ShapeDtypeStruct((1, A), f32), jax.ShapeDtypeStruct((4, 8, C), f32)),
        in_specs=[pl.BlockSpec(memory_space=pl.ANY)] * 12,
        out_specs=(vm, vm),
        scratch_shapes=[
            pltpu.VMEM((4, 8, C), f32),
            pltpu.VMEM((A, C), bf16),
            pltpu.VMEM((1, A), jnp.int32),
            pltpu.VMEM((4, C), bf16),
            pltpu.VMEM((1, C), f32),
            pltpu.VMEM((BRICKS, 32), jnp.int32),
            pltpu.VMEM((K, A), jnp.int32),
            pltpu.VMEM((1, A), jnp.int32),
            pltpu.VMEM((K, A), f32),
            pltpu.VMEM((1, H), f32),
            pltpu.VMEM((1, C), f32),
            pltpu.VMEM((1, A), f32),
            dma((12,)),
            pltpu.VMEM((A, C), f32),
            pltpu.VMEM((T, C), bf16),
            pltpu.VMEM((CELLS, 16, C), bf16),
            pltpu.VMEM((CELLS, 16, C), bf16),
            pltpu.VMEM((BRICKS, 32, C), bf16),
            pltpu.VMEM((rows, 128), jnp.int32),
            pltpu.VMEM((rows, 128), f32),
            pltpu.VMEM((2 * rows, 128), f32),
            pltpu.VMEM((rows, C), bf16),
            pltpu.VMEM((rows, C), bf16),
            pltpu.VMEM((rows, T), f32),
            pltpu.VMEM((rows, 128), f32),
            pltpu.VMEM((8, 128, 1024), bf16),
            pltpu.VMEM((8, T, 1024), bf16),
            pltpu.VMEM((T, rows), bf16),
            pltpu.VMEM((T, rows), bf16),
            pltpu.VMEM((A, 128), jnp.int32),
            pltpu.VMEM((C, T), bf16),
            pltpu.VMEM((2 * C, 128), f32),
            pltpu.VMEM((4, BRICKS, CELLS, C), bf16),
            pltpu.VMEM((4, 16, 16, C), bf16),
            pltpu.VMEM((128, 128), f32),
            pltpu.VMEM((16, 8, 128), bf16),
            pltpu.VMEM((16, 8, 128), bf16),
            pltpu.VMEM((BRICKS * 8, 128), f32),
            dma((4, 16)),
            dma((4, 16)),
            dma((2, BRICKS)),
            dma((4, 2, 16)),
            dma((2, 16)),
            dma((2, BRICKS)),
        ],
        compiler_params=pltpu.CompilerParams(collective_id=0, has_side_effects=True),
        name="step",
    )(*args)


def update_kernel(energy, owned, moment, second, energy_out, moment_out, second_out, step_out):
    g = owned[...]
    m = 0.9 * moment[...] + 0.1 * g
    s = 0.999 * second[...] + 0.001 * g * g
    moment_out[...] = m
    second_out[...] = s
    step_out[...] = m / (jnp.sqrt(s) + 1e-08)
    energy_out[...] = energy[...]


def update(energy, owned, moment, second):
    vm = pl.BlockSpec(memory_space=pltpu.VMEM)
    block = jax.ShapeDtypeStruct((4, 8, C), f32)
    return pl.pallas_call(
        update_kernel,
        out_shape=(jax.ShapeDtypeStruct((1, A), f32), block, block, block),
        in_specs=[vm] * 4,
        out_specs=(vm,) * 4,
        name="update",
    )(energy, owned, moment, second)


def body(features, species, species_table, neighbours, counts, send_lists, distances,
         head_decay, norm_gain, readout, targets, master, moment, second):
    energy, owned = step(
        master, features.reshape(A, C), species.reshape(1, A), species_table,
        norm_gain.reshape(1, C), send_lists.reshape(BRICKS, 32),
        neighbours.reshape(K, A), counts.reshape(1, A), distances.reshape(K, A),
        head_decay.reshape(1, H), readout.reshape(1, C), targets.reshape(1, A))
    energies, moment_new, second_new, adam_step = update(energy, owned, moment, second)
    return (energies.reshape(1, 1, A), moment_new, second_new, adam_step)


def solution(mesh):
    return jax.shard_map(
        body,
        mesh=mesh,
        in_specs=(
            P("cell", "brick", None, None),
            P("cell", "brick", None),
            P(),
            P("cell", "brick", None, None),
            P("cell", "brick", None),
            P("cell", "brick", None, None),
            P("cell", "brick", None, None),
            P(),
            P(),
            P(),
            P("cell", "brick", None),
            P(None, "cell", None),
            P(None, "cell", None),
            P(None, "cell", None),
        ),
        out_specs=(
            P("cell", "brick", None),
            P(None, "cell", None),
            P(None, "cell", None),
            P(None, "cell", None),
        ),
        check_vma=False,
    )
```

```python
import functools
import math

import jax
import jax.numpy as jnp
from jax import lax
from jax.experimental import pallas as pl
from jax.experimental.pallas import tpu as pltpu
from jax.sharding import PartitionSpec as P

MESH = pl.DeviceIdType.MESH
loss_weight = 0.0625
epsilon_norm = 1e-06
C = 256
H = 8
A = 128
K = 64
T = 384
CELLS = 32
BRICKS = 8
f32 = jnp.float32
bf16 = jnp.bfloat16


def dot(a, b, dims):
    return lax.dot_general(a, b, (dims, ((), ())), preferred_element_type=f32)


NN = ((1,), (0,))
NT = ((1,), (1,))
TN = ((0,), (0,))


def split(x):
    hi = x.astype(bf16)
    return hi, (x - hi.astype(f32)).astype(bf16)


def peer(cell, brick):
    return {"cell": cell, "brick": brick}


def step_kernel(master_h, feat_h, spec_h, table_h, gain_h, sends_h, nbr_h, cnt_h, dist_h, decay_h, readout_h, target_h,
                energy, out,
                master, feat, spec, table, gain, sends, nbr, cnt, dist, decay, readout, target, sem_in,
                emb, nt, wa, wb, parcel,
                idx, dst8, rep, qm, gm, qm_t, gm_t, big, att, onehot, p2, msk, k2, v2,
                n_t, gtmp, gsend, r1, s2f, s2, r2, fin,
                sem_a, sem_b, sem_g, sem_1, sem_2, sem_3):
    c = lax.axis_index("cell")
    b = lax.axis_index("brick")
    partner = c + 1 - 2 * lax.rem(c, 2)
    loads = []
    for i, (src, dst) in enumerate((
            (master_h, master), (feat_h, feat), (spec_h, spec), (table_h, table), (gain_h, gain), (sends_h, sends),
            (nbr_h, nbr), (cnt_h, cnt), (dist_h, dist), (decay_h, decay), (readout_h, readout), (target_h, target))):
        cp = pltpu.make_async_copy(src, dst, sem_in.at[i])
        cp.start()
        loads.append(cp)
    barrier = pltpu.get_barrier_semaphore()
    low = lax.rem(c, 16)
    base = c - low
    other = 16 - base

    def at(dz, flip):
        return lax.rem(low + 2 * dz + 16, 16) + (other if flip else base)

    def column(flip):
        return b + 1 - 2 * lax.rem(b, 2) if flip else b

    spots = [(1, 0), (1, 1), (2, 0), (2, 1), (-1, 0), (-1, 1), (-2, 0), (-2, 1), (0, 1)]
    hops = [(2, -1, 0), (2, -1, 1), (2, -2, 0), (2, -2, 1), (-2, 1, 0), (-2, 1, 1)]

    def plane(i):
        return peer(at(0, i // 8), lax.rem(b + i % 8, BRICKS))

    for i in range(1, 16):
        pl.semaphore_signal(barrier, inc=1, device_id=plane(i), device_id_type=MESH)
    for dz, flip in spots[:8]:
        pl.semaphore_signal(barrier, inc=1, device_id=peer(at(dz, flip), column(flip)), device_id_type=MESH)
    pl.semaphore_signal(barrier, inc=1, device_id=peer(partner, b), device_id_type=MESH)
    loads[0].wait()
    wa[c] = master[0:2].reshape(16, C).astype(bf16)
    wb[c] = master[2:4].reshape(16, C).astype(bf16)
    pl.semaphore_wait(barrier, 24)

    def send(w, sem, half, i, block, cell, brick):
        cp = pltpu.make_async_remote_copy(
            src_ref=w.at[block], dst_ref=w.at[block], send_sem=sem.at[half, i], recv_sem=sem.at[half + 1, i],
            device_id=peer(cell, brick), device_id_type=MESH)
        cp.start()
        return cp

    def share(w, sem, i, block):
        return send(w, sem, 2, i, block, partner, b)

    def start_near(w, sem):
        near = [send(w, sem, 0, i, c, at(dz, flip), column(flip)) for i, (dz, flip) in enumerate(spots)]
        return near, [share(w, sem, 15, c)]

    def relay(w, sem, near, shared):
        far = []
        for i, (dz, flip) in enumerate(spots):
            near[i].wait_recv()
            block = at(-dz, flip)
            for j, (to, off, kind) in enumerate(hops):
                if (-dz, flip) == (off, kind):
                    far.append(send(w, sem, 0, 9 + j, block, at(to, 0), b))
            shared.append(share(w, sem, i, block))
        return far

    def finish(w, sem, far, shared):
        for j, (to, off, kind) in enumerate(hops):
            far[j].wait_recv()
            shared.append(share(w, sem, 9 + j, at(off - to, kind)))

    near_a, shared_a = start_near(wa, sem_a)
    for cp in loads[1:6]:
        cp.wait()
    eye = lax.broadcasted_iota(jnp.int32, (A, A), 0) == lax.broadcasted_iota(jnp.int32, (A, A), 1)
    col = jnp.sum(jnp.where(eye, jnp.broadcast_to(spec[...], (A, A)), 0).astype(f32), axis=1, keepdims=True)
    e = feat[...].astype(f32)
    tab = table[...].astype(f32)
    add = jnp.zeros((A, C), f32)
    for s in range(4):
        add = jnp.where(col == float(s), tab[s : s + 1, :], add)
    e = e + add
    emb[...] = e
    rms = lax.rsqrt(jnp.sum(e * e, axis=1, keepdims=True) * (1.0 / C) + epsilon_norm)
    n = (e * rms * gain[...]).astype(bf16)
    nt[0:A, :] = n
    row_id = lax.broadcasted_iota(jnp.int32, (A, 32), 0)
    for d in range(BRICKS):
        take = (row_id == sends[d : d + 1, :]).astype(f32).astype(bf16)
        parcel[d] = dot(take, n, TN).astype(bf16)
    nt[pl.ds(pl.multiple_of(A + 32 * b, 32), 32), :] = parcel[b]
    ghosts = []
    for d in range(1, BRICKS):
        to = lax.rem(b + d, BRICKS)
        cp = pltpu.make_async_remote_copy(
            src_ref=parcel.at[to],
            dst_ref=nt.at[pl.ds(pl.multiple_of(A + 32 * b, 32), 32), :],
            send_sem=sem_g.at[0, d], recv_sem=sem_g.at[1, d],
            device_id=peer(c, to), device_id_type=MESH)
        cp.start()
        ghosts.append(cp)
    near_b, shared_b = start_near(wb, sem_b)
    for cp in loads[6:]:
        cp.wait()

    scale = 1.0 / math.sqrt(C // H)
    rows = A * H
    slot = lax.broadcasted_iota(jnp.int32, (K, A), 0)
    masked = jnp.where(slot < cnt[...], nbr[...], 512)
    m_t = masked.T
    d_t = dist[...].T
    m2 = jnp.concatenate([m_t, m_t], axis=1)
    d2 = jnp.concatenate([d_t, d_t], axis=1)
    msk[...] = jnp.bitwise_and(masked, 127)
    for h in range(H):
        idx[pl.ds(h, A, stride=8), :] = m2
        dst8[pl.ds(h, A, stride=8), :] = d2
    far_a = relay(wa, sem_a, near_a, shared_a)
    far_b = relay(wb, sem_b, near_b, shared_b)
    lane64 = lax.broadcasted_iota(jnp.int32, (K, 128), 1)

    @pl.loop(0, A // 4)
    def _(g):
        for i in range(4):
            column_a = jnp.take_along_axis(msk[...], jnp.full((K, 128), 4 * g + i, jnp.int32), axis=1)
            onehot[g, 64 * i : 64 * i + 64, :] = jnp.where(column_a == lane64, 1.0, 0.0).astype(bf16)

    finish(wa, sem_a, far_a, shared_a)
    for cp in ghosts:
        cp.wait()
    n_cols = nt[...].astype(f32).T.astype(bf16)
    n_t[:, 0:T] = n_cols
    n_t[:, T : 2 * T] = n_cols
    for cp in shared_a:
        cp.wait_recv()

    def weight(w, m):
        return w[:, 8 * m : 8 * m + 8, :].astype(f32).reshape(C, C).astype(bf16)

    n_all = nt[...]
    n_own = nt[0:A, :]
    q = dot(n_own, weight(wa, 0), NN).astype(bf16)
    k = dot(n_all, weight(wa, 1), NN).astype(bf16)

    head_of_lane = lax.broadcasted_iota(jnp.int32, (rows, C), 1) // 32
    head_of_row = lax.rem(lax.broadcasted_iota(jnp.int32, (rows, C), 0), 8)
    head_mask = head_of_lane == head_of_row

    def spread_heads(x32):
        for h in range(H):
            rep[pl.ds(h, A, stride=8), :] = x32[:, 0:128]
            rep[pl.ds(rows + h, A, stride=8), :] = x32[:, 128:256]
        x = jnp.concatenate([rep[0:rows, :], rep[rows : 2 * rows, :]], axis=1)
        return jnp.where(head_mask, x, 0.0).astype(bf16)

    qm[...] = spread_heads(q.astype(f32))
    qm_t[...] = qm[...].T
    big[...] = dot(qm[...], k, NT)
    finish(wb, sem_b, far_b, shared_b)

    lane = lax.broadcasted_iota(jnp.int32, (128, 128), 1)
    row_in = lax.broadcasted_iota(jnp.int32, (128, 128), 0)
    sub_head = lax.rem(row_in, 8)
    dec = jnp.zeros((128, 128), f32)
    for h in range(H):
        dec = jnp.where(sub_head == h, decay[:, h : h + 1], dec)
    diag = lax.rem(row_in // 8, 2) == lane // 64

    def pick(s):
        r0 = s * 128
        ix = idx[pl.ds(r0, 128), :]
        low = jnp.bitwise_and(ix, 127)
        res = jnp.zeros((128, 128), f32)
        for t in range(3):
            g = jnp.take_along_axis(big[pl.ds(r0, 128), 128 * t : 128 * t + 128], low, axis=1)
            res = jnp.where(ix >= 128 * t, g, res)
        return res, ix < 512

    blank = jnp.zeros((16, 128), bf16)

    def scatter(s, w32):
        kept = jnp.where(diag, w32, 0.0)
        block = idx[128 * s : 128 * s + 128, :] // 128
        parts = [jnp.where(block == t, kept, 0.0).astype(bf16) for t in range(3)]
        dense = []
        for i in range(4):
            r = 32 * i
            left = jnp.concatenate([x[r : r + 16, :] if y == 0 else blank for x in parts for y in range(2)], axis=0)
            right = jnp.concatenate([blank if y == 0 else x[r + 16 : r + 32, :] for x in parts for y in range(2)], axis=0)
            dense.append(dot(jnp.concatenate([left, right], axis=1), onehot[4 * s + i], NN))
        for t in range(3):
            x = jnp.concatenate([d[32 * t : 32 * t + 32, :] for d in dense], axis=0)
            hi, lo = split(x)
            p2[128 * s : 128 * s + 128, 128 * t : 128 * t + 128] = hi
            p2[128 * s : 128 * s + 128, T + 128 * t : T + 128 * t + 128] = lo

    for s in range(8):
        r0 = s * 128
        got, ok = pick(s)
        score = got * scale - dec * dst8[pl.ds(r0, 128), :]
        score = jnp.where(ok, score, -1e30)
        top = jnp.max(score, axis=1, keepdims=True)
        ex = jnp.where(ok, jnp.exp(score - top), 0.0)
        a = ex / (jnp.sum(ex, axis=1, keepdims=True) * 0.5)
        att[pl.ds(r0, 128), :] = a
        scatter(s, a)

    for cp in shared_b:
        cp.wait_recv()
    w_o = weight(wb, 1)
    v = dot(n_all, weight(wb, 0), NN).astype(bf16)

    collect = (lax.broadcasted_iota(jnp.int32, (A, rows), 1) // 8
               == lax.broadcasted_iota(jnp.int32, (A, rows), 0)).astype(f32).astype(bf16)

    def gather_heads(source, mult):
        full = dot(p2[...], source[...], NN)
        if mult is not None:
            full = full * mult
        kept = jnp.where(head_mask, full, 0.0).astype(bf16)
        return dot(collect, kept, NN).astype(bf16)

    v2[0:T, :] = v
    v2[T : 2 * T, :] = v
    k2[0:T, :] = k
    k2[T : 2 * T, :] = k
    attended = gather_heads(v2, None)
    updated = emb[...] + dot(attended, w_o, NN)
    sig = jax.nn.sigmoid(updated)
    e_col = jnp.sum(readout[...] * (updated * sig), axis=1, keepdims=True)
    energy[...] = jnp.sum(jnp.where(eye, e_col, 0.0), axis=0, keepdims=True)
    t_col = jnp.sum(jnp.where(eye, target[...], 0.0), axis=1, keepdims=True)
    grad_energy = loss_weight * (e_col - t_col)
    slope = sig * (1.0 + updated * (1.0 - sig))
    grad_updated = (grad_energy * readout[...] * slope).astype(bf16)
    grad_att = dot(grad_updated, w_o, NT).astype(bf16)

    first = [None] * 4

    def put(m, x):
        gtmp[0:C, :] = x[:, 0:128]
        gtmp[C : 2 * C, :] = x[:, 128:256]
        for d in range(BRICKS):
            gsend[m, d] = jnp.concatenate(
                [gtmp[pl.ds(d, CELLS, stride=8), :], gtmp[pl.ds(C + d, CELLS, stride=8), :]], axis=1).astype(bf16)
        made = []
        for i in range(1, 16):
            half = pl.ds(pl.multiple_of(other if i // 8 else base, 16), 16)
            cp = pltpu.make_async_remote_copy(
                src_ref=gsend.at[m, lax.rem(b + i % 8, BRICKS), half, :], dst_ref=r1.at[m, base // 2 + b],
                send_sem=sem_1.at[m, 0, i], recv_sem=sem_1.at[m, 1, i],
                device_id=plane(i), device_id_type=MESH)
            cp.start()
            made.append(cp)
        first[m] = made

    put(3, dot(attended, grad_updated, TN))
    gm[...] = spread_heads(grad_att.astype(f32))
    gm_t[...] = gm[...].T
    big[...] = dot(gm[...], v, NT)

    def table_grad(rows_t, mult):
        both = dot(rows_t, p2[...], NN)
        tg = both[:, 0:T] + both[:, T : 2 * T]
        if mult is not None:
            tg = tg * mult
        return dot(n_t[...], jnp.concatenate(split(tg), axis=1), NT)

    put(2, table_grad(gm_t[...], None))

    for s in range(8):
        r0 = s * 128
        gw, ok = pick(s)
        a = att[pl.ds(r0, 128), :]
        mean = jnp.sum(a * gw, axis=1, keepdims=True) * 0.5
        scatter(s, a * (gw - mean))

    put(1, table_grad(qm_t[...], scale))
    grad_query = gather_heads(k2, scale)
    put(0, dot(n_t[:, 0:A], grad_query, NN))

    for m in (3, 2, 1, 0):
        total = gsend[m, b, pl.ds(pl.multiple_of(base, 16), 16), :].astype(f32)
        for i in range(1, 16):
            first[m][i - 1].wait_recv()
            source = (other if i // 8 else base) // 2 + lax.rem(b - i % 8 + BRICKS, BRICKS)
            total = total + r1[m, source].astype(f32)
        s2f[pl.ds(2 * m, 16, stride=8), :] = total[:, 0:128]
        s2f[pl.ds(2 * m + 1, 16, stride=8), :] = total[:, 128:256]
    s2[...] = s2f[...].reshape(16, 8, 128).astype(bf16)

    second = []
    for k in range(1, 16):
        to = lax.rem(low + k, 16)
        cp = pltpu.make_async_remote_copy(
            src_ref=s2.at[to], dst_ref=r2.at[low], send_sem=sem_2.at[0, k], recv_sem=sem_2.at[1, k],
            device_id=peer(base + to, b), device_id_type=MESH)
        cp.start()
        second.append(cp)
    r2[low] = s2[low]
    for cp in near_a + near_b + far_a + far_b + shared_a + shared_b:
        cp.wait_send()
    for m in range(4):
        for cp in first[m]:
            cp.wait_send()
    for cp in second:
        cp.wait_recv()
    mine = pl.ds(pl.multiple_of(8 * b, 8), 8)
    fin[mine, :] = jnp.sum(r2[...].astype(f32), axis=0)

    third = []
    for d in range(1, BRICKS):
        cp = pltpu.make_async_remote_copy(
            src_ref=fin.at[mine, :], dst_ref=fin.at[mine, :], send_sem=sem_3.at[0, d], recv_sem=sem_3.at[1, d],
            device_id=peer(c, lax.rem(b + d, BRICKS)), device_id_type=MESH)
        cp.start()
        third.append(cp)
    for cp in second:
        cp.wait_send()
    for cp in third:
        cp.wait()
    for m in range(4):
        out[m] = jnp.concatenate([fin[pl.ds(2 * m, 8, stride=8), :], fin[pl.ds(2 * m + 1, 8, stride=8), :]], axis=1)


def step(*args):
    vm = pl.BlockSpec(memory_space=pltpu.VMEM)
    rows = A * H
    dma = pltpu.SemaphoreType.DMA
    return pl.pallas_call(
        step_kernel,
        out_shape=(jax.ShapeDtypeStruct((1, A), f32), jax.ShapeDtypeStruct((4, 8, C), f32)),
        in_specs=[pl.BlockSpec(memory_space=pl.ANY)] * 12,
        out_specs=(vm, vm),
        scratch_shapes=[
            pltpu.VMEM((4, 8, C), f32),
            pltpu.VMEM((A, C), bf16),
            pltpu.VMEM((1, A), jnp.int32),
            pltpu.VMEM((4, C), bf16),
            pltpu.VMEM((1, C), f32),
            pltpu.VMEM((BRICKS, 32), jnp.int32),
            pltpu.VMEM((K, A), jnp.int32),
            pltpu.VMEM((1, A), jnp.int32),
            pltpu.VMEM((K, A), f32),
            pltpu.VMEM((1, H), f32),
            pltpu.VMEM((1, C), f32),
            pltpu.VMEM((1, A), f32),
            dma((12,)),
            pltpu.VMEM((A, C), f32),
            pltpu.VMEM((T, C), bf16),
            pltpu.VMEM((CELLS, 16, C), bf16),
            pltpu.VMEM((CELLS, 16, C), bf16),
            pltpu.VMEM((BRICKS, 32, C), bf16),
            pltpu.VMEM((rows, 128), jnp.int32),
            pltpu.VMEM((rows, 128), f32),
            pltpu.VMEM((2 * rows, 128), f32),
            pltpu.VMEM((rows, C), bf16),
            pltpu.VMEM((rows, C), bf16),
            pltpu.VMEM((C, rows), bf16),
            pltpu.VMEM((C, rows), bf16),
            pltpu.VMEM((rows, T), f32),
            pltpu.VMEM((rows, 128), f32),
            pltpu.VMEM((A // 4, 256, 128), bf16),
            pltpu.VMEM((rows, 2 * T), bf16),
            pltpu.VMEM((K, A), jnp.int32),
            pltpu.VMEM((2 * T, C), bf16),
            pltpu.VMEM((2 * T, C), bf16),
            pltpu.VMEM((C, 2 * T), bf16),
            pltpu.VMEM((2 * C, 128), f32),
            pltpu.VMEM((4, BRICKS, CELLS, C), bf16),
            pltpu.VMEM((4, 16, 16, C), bf16),
            pltpu.VMEM((128, 128), f32),
            pltpu.VMEM((16, 8, 128), bf16),
            pltpu.VMEM((16, 8, 128), bf16),
            pltpu.VMEM((BRICKS * 8, 128), f32),
            dma((4, 16)),
            dma((4, 16)),
            dma((2, BRICKS)),
            dma((4, 2, 16)),
            dma((2, 16)),
            dma((2, BRICKS)),
        ],
        compiler_params=pltpu.CompilerParams(collective_id=0, has_side_effects=True),
        name="step",
    )(*args)


def update_kernel(energy, owned, moment, second, energy_out, moment_out, second_out, step_out):
    g = owned[...]
    m = 0.9 * moment[...] + 0.1 * g
    s = 0.999 * second[...] + 0.001 * g * g
    moment_out[...] = m
    second_out[...] = s
    step_out[...] = m / (jnp.sqrt(s) + 1e-08)
    energy_out[...] = energy[...]


def update(energy, owned, moment, second):
    vm = pl.BlockSpec(memory_space=pltpu.VMEM)
    block = jax.ShapeDtypeStruct((4, 8, C), f32)
    return pl.pallas_call(
        update_kernel,
        out_shape=(jax.ShapeDtypeStruct((1, A), f32), block, block, block),
        in_specs=[vm] * 4,
        out_specs=(vm,) * 4,
        name="update",
    )(energy, owned, moment, second)


def body(features, species, species_table, neighbours, counts, send_lists, distances,
         head_decay, norm_gain, readout, targets, master, moment, second):
    energy, owned = step(
        master, features.reshape(A, C), species.reshape(1, A), species_table,
        norm_gain.reshape(1, C), send_lists.reshape(BRICKS, 32),
        neighbours.reshape(K, A), counts.reshape(1, A), distances.reshape(K, A),
        head_decay.reshape(1, H), readout.reshape(1, C), targets.reshape(1, A))
    energies, moment_new, second_new, adam_step = update(energy, owned, moment, second)
    return (energies.reshape(1, 1, A), moment_new, second_new, adam_step)


def solution(mesh):
    return jax.shard_map(
        body,
        mesh=mesh,
        in_specs=(
            P("cell", "brick", None, None),
            P("cell", "brick", None),
            P(),
            P("cell", "brick", None, None),
            P("cell", "brick", None),
            P("cell", "brick", None, None),
            P("cell", "brick", None, None),
            P(),
            P(),
            P(),
            P("cell", "brick", None),
            P(None, "cell", None),
            P(None, "cell", None),
            P(None, "cell", None),
        ),
        out_specs=(
            P("cell", "brick", None),
            P(None, "cell", None),
            P(None, "cell", None),
            P(None, "cell", None),
        ),
        check_vma=False,
    )
```

```python
import functools
import math

import jax
import jax.numpy as jnp
from jax import lax
from jax.experimental import pallas as pl
from jax.experimental.pallas import tpu as pltpu
from jax.sharding import PartitionSpec as P

MESH = pl.DeviceIdType.MESH
loss_weight = 0.0625
epsilon_norm = 1e-06
C = 256
H = 8
A = 128
K = 64
T = 384
CELLS = 32
BRICKS = 8
f32 = jnp.float32
bf16 = jnp.bfloat16


def dot(a, b, dims):
    return lax.dot_general(a, b, (dims, ((), ())), preferred_element_type=f32)


NN = ((1,), (0,))
NT = ((1,), (1,))
TN = ((0,), (0,))


def split(x):
    hi = x.astype(bf16)
    return hi, (x - hi.astype(f32)).astype(bf16)


def peer(cell, brick):
    return {"cell": cell, "brick": brick}


def step_kernel(master_h, feat_h, spec_h, table_h, gain_h, sends_h, nbr_h, cnt_h, dist_h, decay_h, readout_h, target_h,
                energy, out,
                master, feat, spec, table, gain, sends, nbr, cnt, dist, decay, readout, target, sem_in,
                emb, nt, wa, wb, parcel,
                idx, dst8, rep, qm, gm, qm_t, gm_t, big, att, onehot, p2, msk, k2, v2,
                n_t, gtmp, gsend, r1, s2f, s2, r2, fin,
                sem_a, sem_b, sem_g, sem_1, sem_2, sem_3):
    c = lax.axis_index("cell")
    b = lax.axis_index("brick")
    partner = c + 1 - 2 * lax.rem(c, 2)
    loads = []
    for i, (src, dst) in enumerate((
            (master_h, master), (feat_h, feat), (spec_h, spec), (table_h, table), (gain_h, gain), (sends_h, sends),
            (nbr_h, nbr), (cnt_h, cnt), (dist_h, dist), (decay_h, decay), (readout_h, readout), (target_h, target))):
        cp = pltpu.make_async_copy(src, dst, sem_in.at[i])
        cp.start()
        loads.append(cp)
    barrier = pltpu.get_barrier_semaphore()
    low = lax.rem(c, 16)
    base = c - low
    other = 16 - base

    def at(dz, flip):
        return lax.rem(low + 2 * dz + 16, 16) + (other if flip else base)

    def column(flip):
        return b + 1 - 2 * lax.rem(b, 2) if flip else b

    spots = [(1, 0), (1, 1), (2, 0), (2, 1), (-1, 0), (-1, 1), (-2, 0), (-2, 1), (0, 1)]
    hops = [(2, -1, 0), (2, -1, 1), (2, -2, 0), (2, -2, 1), (-2, 1, 0), (-2, 1, 1)]

    def plane(i):
        return peer(at(0, i // 8), lax.rem(b + i % 8, BRICKS))

    for i in range(1, 16):
        pl.semaphore_signal(barrier, inc=1, device_id=plane(i), device_id_type=MESH)
    for dz, flip in spots[:8]:
        pl.semaphore_signal(barrier, inc=1, device_id=peer(at(dz, flip), column(flip)), device_id_type=MESH)
    pl.semaphore_signal(barrier, inc=1, device_id=peer(partner, b), device_id_type=MESH)
    loads[0].wait()
    wa[c] = master[0:2].reshape(16, C).astype(bf16)
    wb[c] = master[2:4].reshape(16, C).astype(bf16)
    pl.semaphore_wait(barrier, 24)

    def send(w, sem, half, i, block, cell, brick):
        cp = pltpu.make_async_remote_copy(
            src_ref=w.at[block], dst_ref=w.at[block], send_sem=sem.at[half, i], recv_sem=sem.at[half + 1, i],
            device_id=peer(cell, brick), device_id_type=MESH)
        cp.start()
        return cp

    def share(w, sem, i, block):
        return send(w, sem, 2, i, block, partner, b)

    def start_near(w, sem):
        near = [send(w, sem, 0, i, c, at(dz, flip), column(flip)) for i, (dz, flip) in enumerate(spots)]
        return near, [share(w, sem, 15, c)]

    def relay(w, sem, near, shared):
        far = []
        for i, (dz, flip) in enumerate(spots):
            near[i].wait_recv()
            block = at(-dz, flip)
            for j, (to, off, kind) in enumerate(hops):
                if (-dz, flip) == (off, kind):
                    far.append(send(w, sem, 0, 9 + j, block, at(to, 0), b))
            shared.append(share(w, sem, i, block))
        return far

    def finish(w, sem, far, shared):
        for j, (to, off, kind) in enumerate(hops):
            far[j].wait_recv()
            shared.append(share(w, sem, 9 + j, at(off - to, kind)))

    near_a, shared_a = start_near(wa, sem_a)
    for cp in loads[1:6]:
        cp.wait()
    eye = lax.broadcasted_iota(jnp.int32, (A, A), 0) == lax.broadcasted_iota(jnp.int32, (A, A), 1)
    col = jnp.sum(jnp.where(eye, jnp.broadcast_to(spec[...], (A, A)), 0).astype(f32), axis=1, keepdims=True)
    e = feat[...].astype(f32)
    tab = table[...].astype(f32)
    add = jnp.zeros((A, C), f32)
    for s in range(4):
        add = jnp.where(col == float(s), tab[s : s + 1, :], add)
    e = e + add
    emb[...] = e
    rms = lax.rsqrt(jnp.sum(e * e, axis=1, keepdims=True) * (1.0 / C) + epsilon_norm)
    n = (e * rms * gain[...]).astype(bf16)
    nt[0:A, :] = n
    row_id = lax.broadcasted_iota(jnp.int32, (A, 32), 0)
    for d in range(BRICKS):
        take = (row_id == sends[d : d + 1, :]).astype(f32).astype(bf16)
        parcel[d] = dot(take, n, TN).astype(bf16)
    nt[pl.ds(pl.multiple_of(A + 32 * b, 32), 32), :] = parcel[b]
    ghosts = []
    for d in range(1, BRICKS):
        to = lax.rem(b + d, BRICKS)
        cp = pltpu.make_async_remote_copy(
            src_ref=parcel.at[to],
            dst_ref=nt.at[pl.ds(pl.multiple_of(A + 32 * b, 32), 32), :],
            send_sem=sem_g.at[0, d], recv_sem=sem_g.at[1, d],
            device_id=peer(c, to), device_id_type=MESH)
        cp.start()
        ghosts.append(cp)
    near_b, shared_b = start_near(wb, sem_b)
    for cp in loads[6:]:
        cp.wait()

    scale = 1.0 / math.sqrt(C // H)
    rows = A * H
    slot = lax.broadcasted_iota(jnp.int32, (K, A), 0)
    masked = jnp.where(slot < cnt[...], nbr[...], 512)
    m_t = masked.T
    d_t = dist[...].T
    m2 = jnp.concatenate([m_t, m_t], axis=1)
    d2 = jnp.concatenate([d_t, d_t], axis=1)
    msk[...] = jnp.bitwise_and(masked, 127)
    for h in range(H):
        idx[pl.ds(h, A, stride=8), :] = m2
        dst8[pl.ds(h, A, stride=8), :] = d2
    far_a = relay(wa, sem_a, near_a, shared_a)
    far_b = relay(wb, sem_b, near_b, shared_b)
    lane64 = lax.broadcasted_iota(jnp.int32, (K, 128), 1)

    @pl.loop(0, A // 4)
    def _(g):
        for i in range(4):
            column_a = jnp.take_along_axis(msk[...], jnp.full((K, 128), 4 * g + i, jnp.int32), axis=1)
            onehot[g, 64 * i : 64 * i + 64, :] = jnp.where(column_a == lane64, 1.0, 0.0).astype(bf16)

    finish(wa, sem_a, far_a, shared_a)
    for cp in ghosts:
        cp.wait()
    n_cols = nt[...].astype(f32).T.astype(bf16)
    n_t[:, 0:T] = n_cols
    n_t[:, T : 2 * T] = n_cols
    for cp in shared_a:
        cp.wait_recv()

    def weight(w, m):
        return w[:, 8 * m : 8 * m + 8, :].astype(f32).reshape(C, C).astype(bf16)

    n_all = nt[...]
    n_own = nt[0:A, :]
    q = dot(n_own, weight(wa, 0), NN).astype(bf16)
    k = dot(n_all, weight(wa, 1), NN).astype(bf16)

    head_of_lane = lax.broadcasted_iota(jnp.int32, (rows, C), 1) // 32
    head_of_row = lax.rem(lax.broadcasted_iota(jnp.int32, (rows, C), 0), 8)
    head_mask = head_of_lane == head_of_row

    def spread_heads(x32):
        for h in range(H):
            rep[pl.ds(h, A, stride=8), :] = x32[:, 0:128]
            rep[pl.ds(rows + h, A, stride=8), :] = x32[:, 128:256]
        x = jnp.concatenate([rep[0:rows, :], rep[rows : 2 * rows, :]], axis=1)
        return jnp.where(head_mask, x, 0.0).astype(bf16)

    qm[...] = spread_heads(q.astype(f32))
    qm_t[...] = qm[...].T
    big[...] = dot(qm[...], k, NT)
    finish(wb, sem_b, far_b, shared_b)

    lane = lax.broadcasted_iota(jnp.int32, (128, 128), 1)
    row_in = lax.broadcasted_iota(jnp.int32, (128, 128), 0)
    sub_head = lax.rem(row_in, 8)
    dec = jnp.zeros((128, 128), f32)
    for h in range(H):
        dec = jnp.where(sub_head == h, decay[:, h : h + 1], dec)
    diag = lax.rem(row_in // 8, 2) == lane // 64

    def pick(s):
        r0 = s * 128
        ix = idx[pl.ds(r0, 128), :]
        low = jnp.bitwise_and(ix, 127)
        res = jnp.zeros((128, 128), f32)
        for t in range(3):
            g = jnp.take_along_axis(big[pl.ds(r0, 128), 128 * t : 128 * t + 128], low, axis=1)
            res = jnp.where(ix >= 128 * t, g, res)
        return res, ix < 512

    blank = jnp.zeros((16, 128), bf16)

    def scatter(s, w32):
        kept = jnp.where(diag, w32, 0.0)
        block = idx[128 * s : 128 * s + 128, :] // 128
        parts = [jnp.where(block == t, kept, 0.0).astype(bf16) for t in range(3)]
        dense = []
        for i in range(4):
            r = 32 * i
            left = jnp.concatenate([x[r : r + 16, :] if y == 0 else blank for x in parts for y in range(2)], axis=0)
            right = jnp.concatenate([blank if y == 0 else x[r + 16 : r + 32, :] for x in parts for y in range(2)], axis=0)
            dense.append(dot(jnp.concatenate([left, right], axis=1), onehot[4 * s + i], NN))
        for t in range(3):
            x = jnp.concatenate([d[32 * t : 32 * t + 32, :] for d in dense], axis=0)
            hi, lo = split(x)
            p2[128 * s : 128 * s + 128, 128 * t : 128 * t + 128] = hi
            p2[128 * s : 128 * s + 128, T + 128 * t : T + 128 * t + 128] = lo

    for s in range(8):
        r0 = s * 128
        got, ok = pick(s)
        score = got * scale - dec * dst8[pl.ds(r0, 128), :]
        score = jnp.where(ok, score, -1e30)
        top = jnp.max(score, axis=1, keepdims=True)
        ex = jnp.where(ok, jnp.exp(score - top), 0.0)
        a = ex / (jnp.sum(ex, axis=1, keepdims=True) * 0.5)
        att[pl.ds(r0, 128), :] = a
        scatter(s, a)

    for cp in shared_b:
        cp.wait_recv()
    w_o = weight(wb, 1)
    v = dot(n_all, weight(wb, 0), NN).astype(bf16)

    collect = (lax.broadcasted_iota(jnp.int32, (A, rows), 1) // 8
               == lax.broadcasted_iota(jnp.int32, (A, rows), 0)).astype(f32).astype(bf16)

    def gather_heads(source, mult):
        full = dot(p2[...], source[...], NN)
        if mult is not None:
            full = full * mult
        kept = jnp.where(head_mask, full, 0.0).astype(bf16)
        return dot(collect, kept, NN).astype(bf16)

    v2[0:T, :] = v
    v2[T : 2 * T, :] = v
    k2[0:T, :] = k
    k2[T : 2 * T, :] = k
    attended = gather_heads(v2, None)
    updated = emb[...] + dot(attended, w_o, NN)
    sig = jax.nn.sigmoid(updated)
    e_col = jnp.sum(readout[...] * (updated * sig), axis=1, keepdims=True)
    energy[...] = jnp.sum(jnp.where(eye, e_col, 0.0), axis=0, keepdims=True)
    t_col = jnp.sum(jnp.where(eye, target[...], 0.0), axis=1, keepdims=True)
    grad_energy = loss_weight * (e_col - t_col)
    slope = sig * (1.0 + updated * (1.0 - sig))
    grad_updated = (grad_energy * readout[...] * slope).astype(bf16)
    grad_att = dot(grad_updated, w_o, NT).astype(bf16)

    first = [None] * 4

    def put(m, x):
        gtmp[0:C, :] = x[:, 0:128]
        gtmp[C : 2 * C, :] = x[:, 128:256]
        for d in range(BRICKS):
            gsend[m, d] = jnp.concatenate(
                [gtmp[pl.ds(d, CELLS, stride=8), :], gtmp[pl.ds(C + d, CELLS, stride=8), :]], axis=1).astype(bf16)
        made = []
        for i in range(1, 16):
            half = pl.ds(pl.multiple_of(other if i // 8 else base, 16), 16)
            cp = pltpu.make_async_remote_copy(
                src_ref=gsend.at[m, lax.rem(b + i % 8, BRICKS), half, :], dst_ref=r1.at[m, base // 2 + b],
                send_sem=sem_1.at[m, 0, i], recv_sem=sem_1.at[m, 1, i],
                device_id=plane(i), device_id_type=MESH)
            cp.start()
            made.append(cp)
        first[m] = made

    put(3, dot(attended, grad_updated, TN))
    gm[...] = spread_heads(grad_att.astype(f32))
    gm_t[...] = gm[...].T
    big[...] = dot(gm[...], v, NT)

    def table_grad(rows_t, mult):
        both = dot(rows_t, p2[...], NN)
        tg = both[:, 0:T] + both[:, T : 2 * T]
        if mult is not None:
            tg = tg * mult
        return dot(n_t[...], jnp.concatenate(split(tg), axis=1), NT)

    put(2, table_grad(gm_t[...], None))

    for s in range(8):
        r0 = s * 128
        gw, ok = pick(s)
        a = att[pl.ds(r0, 128), :]
        mean = jnp.sum(a * gw, axis=1, keepdims=True) * 0.5
        scatter(s, a * (gw - mean))

    put(1, table_grad(qm_t[...], scale))
    grad_query = gather_heads(k2, scale)
    put(0, dot(n_t[:, 0:A], grad_query, NN))

    for m in (3, 2, 1, 0):
        total = gsend[m, b, pl.ds(pl.multiple_of(base, 16), 16), :].astype(f32)
        for i in range(1, 16):
            first[m][i - 1].wait_recv()
            source = (other if i // 8 else base) // 2 + lax.rem(b - i % 8 + BRICKS, BRICKS)
            total = total + r1[m, source].astype(f32)
        s2f[pl.ds(2 * m, 16, stride=8), :] = total[:, 0:128]
        s2f[pl.ds(2 * m + 1, 16, stride=8), :] = total[:, 128:256]
    s2[...] = s2f[...].reshape(16, 8, 128).astype(bf16)

    second = []
    for k in range(1, 16):
        to = lax.rem(low + k, 16)
        cp = pltpu.make_async_remote_copy(
            src_ref=s2.at[to], dst_ref=r2.at[low], send_sem=sem_2.at[0, k], recv_sem=sem_2.at[1, k],
            device_id=peer(base + to, b), device_id_type=MESH)
        cp.start()
        second.append(cp)
    r2[low] = s2[low]
    for cp in near_a + near_b + far_a + far_b + shared_a + shared_b:
        cp.wait_send()
    for m in range(4):
        for cp in first[m]:
            cp.wait_send()
    for cp in second:
        cp.wait_recv()
    mine = pl.ds(pl.multiple_of(8 * b, 8), 8)
    fin[mine, :] = jnp.sum(r2[...].astype(f32), axis=0)

    third = []
    for d in range(1, BRICKS):
        cp = pltpu.make_async_remote_copy(
            src_ref=fin.at[mine, :], dst_ref=fin.at[mine, :], send_sem=sem_3.at[0, d], recv_sem=sem_3.at[1, d],
            device_id=peer(c, lax.rem(b + d, BRICKS)), device_id_type=MESH)
        cp.start()
        third.append(cp)
    for cp in second:
        cp.wait_send()
    for cp in third:
        cp.wait()
    for m in range(4):
        out[m] = jnp.concatenate([fin[pl.ds(2 * m, 8, stride=8), :], fin[pl.ds(2 * m + 1, 8, stride=8), :]], axis=1)


def step(*args):
    vm = pl.BlockSpec(memory_space=pltpu.VMEM)
    rows = A * H
    dma = pltpu.SemaphoreType.DMA
    return pl.pallas_call(
        step_kernel,
        out_shape=(pltpu.VMEM((1, A), f32), pltpu.VMEM((4, 8, C), f32)),
        in_specs=[pl.BlockSpec(memory_space=pl.ANY)] * 12,
        out_specs=(vm, vm),
        scratch_shapes=[
            pltpu.VMEM((4, 8, C), f32),
            pltpu.VMEM((A, C), bf16),
            pltpu.VMEM((1, A), jnp.int32),
            pltpu.VMEM((4, C), bf16),
            pltpu.VMEM((1, C), f32),
            pltpu.VMEM((BRICKS, 32), jnp.int32),
            pltpu.VMEM((K, A), jnp.int32),
            pltpu.VMEM((1, A), jnp.int32),
            pltpu.VMEM((K, A), f32),
            pltpu.VMEM((1, H), f32),
            pltpu.VMEM((1, C), f32),
            pltpu.VMEM((1, A), f32),
            dma((12,)),
            pltpu.VMEM((A, C), f32),
            pltpu.VMEM((T, C), bf16),
            pltpu.VMEM((CELLS, 16, C), bf16),
            pltpu.VMEM((CELLS, 16, C), bf16),
            pltpu.VMEM((BRICKS, 32, C), bf16),
            pltpu.VMEM((rows, 128), jnp.int32),
            pltpu.VMEM((rows, 128), f32),
            pltpu.VMEM((2 * rows, 128), f32),
            pltpu.VMEM((rows, C), bf16),
            pltpu.VMEM((rows, C), bf16),
            pltpu.VMEM((C, rows), bf16),
            pltpu.VMEM((C, rows), bf16),
            pltpu.VMEM((rows, T), f32),
            pltpu.VMEM((rows, 128), f32),
            pltpu.VMEM((A // 4, 256, 128), bf16),
            pltpu.VMEM((rows, 2 * T), bf16),
            pltpu.VMEM((K, A), jnp.int32),
            pltpu.VMEM((2 * T, C), bf16),
            pltpu.VMEM((2 * T, C), bf16),
            pltpu.VMEM((C, 2 * T), bf16),
            pltpu.VMEM((2 * C, 128), f32),
            pltpu.VMEM((4, BRICKS, CELLS, C), bf16),
            pltpu.VMEM((4, 16, 16, C), bf16),
            pltpu.VMEM((128, 128), f32),
            pltpu.VMEM((16, 8, 128), bf16),
            pltpu.VMEM((16, 8, 128), bf16),
            pltpu.VMEM((BRICKS * 8, 128), f32),
            dma((4, 16)),
            dma((4, 16)),
            dma((2, BRICKS)),
            dma((4, 2, 16)),
            dma((2, 16)),
            dma((2, BRICKS)),
        ],
        compiler_params=pltpu.CompilerParams(collective_id=0, has_side_effects=True),
        name="step",
    )(*args)


def update_kernel(energy, owned, moment, second, energy_out, moment_out, second_out, step_out):
    g = owned[...]
    m = 0.9 * moment[...] + 0.1 * g
    s = 0.999 * second[...] + 0.001 * g * g
    moment_out[...] = m
    second_out[...] = s
    step_out[...] = m / (jnp.sqrt(s) + 1e-08)
    energy_out[...] = energy[...]


def update(energy, owned, moment, second):
    vm = pl.BlockSpec(memory_space=pltpu.VMEM)
    block = jax.ShapeDtypeStruct((4, 8, C), f32)
    energy = pltpu.with_memory_space_constraint(energy, pltpu.VMEM)
    owned = pltpu.with_memory_space_constraint(owned, pltpu.VMEM)
    moment = pltpu.with_memory_space_constraint(moment, pltpu.VMEM)
    second = pltpu.with_memory_space_constraint(second, pltpu.VMEM)
    return pl.pallas_call(
        update_kernel,
        out_shape=(jax.ShapeDtypeStruct((1, A), f32), block, block, block),
        in_specs=[vm] * 4,
        out_specs=(vm,) * 4,
        name="update",
    )(energy, owned, moment, second)


def body(features, species, species_table, neighbours, counts, send_lists, distances,
         head_decay, norm_gain, readout, targets, master, moment, second):
    energy, owned = step(
        master, features.reshape(A, C), species.reshape(1, A), species_table,
        norm_gain.reshape(1, C), send_lists.reshape(BRICKS, 32),
        neighbours.reshape(K, A), counts.reshape(1, A), distances.reshape(K, A),
        head_decay.reshape(1, H), readout.reshape(1, C), targets.reshape(1, A))
    energies, moment_new, second_new, adam_step = update(energy, owned, moment, second)
    return (energies.reshape(1, 1, A), moment_new, second_new, adam_step)


def solution(mesh):
    return jax.shard_map(
        body,
        mesh=mesh,
        in_specs=(
            P("cell", "brick", None, None),
            P("cell", "brick", None),
            P(),
            P("cell", "brick", None, None),
            P("cell", "brick", None),
            P("cell", "brick", None, None),
            P("cell", "brick", None, None),
            P(),
            P(),
            P(),
            P("cell", "brick", None),
            P(None, "cell", None),
            P(None, "cell", None),
            P(None, "cell", None),
        ),
        out_specs=(
            P("cell", "brick", None),
            P(None, "cell", None),
            P(None, "cell", None),
            P(None, "cell", None),
        ),
        check_vma=False,
    )
```

```python
import functools
import math

import jax
import jax.numpy as jnp
from jax import lax
from jax.experimental import pallas as pl
from jax.experimental.pallas import tpu as pltpu
from jax.sharding import PartitionSpec as P

MESH = pl.DeviceIdType.MESH
loss_weight = 0.0625
epsilon_norm = 1e-06
C = 256
H = 8
A = 128
K = 64
T = 384
CELLS = 32
BRICKS = 8
f32 = jnp.float32
bf16 = jnp.bfloat16


def dot(a, b, dims):
    return lax.dot_general(a, b, (dims, ((), ())), preferred_element_type=f32)


NN = ((1,), (0,))
NT = ((1,), (1,))
TN = ((0,), (0,))


def split(x):
    hi = x.astype(bf16)
    return hi, (x - hi.astype(f32)).astype(bf16)


def peer(cell, brick):
    return {"cell": cell, "brick": brick}


def step_kernel(master_h, feat_h, spec_h, table_h, gain_h, sends_h, nbr_h, cnt_h, dist_h, decay_h, readout_h, target_h,
                energy, out,
                master, feat, spec, table, gain, sends, nbr, cnt, dist, decay, readout, target, sem_in,
                emb, nt, wa, wb, parcel,
                idx, dst8, rep, qm, gm, qm_t, gm_t, big, att, onehot, p2, msk, k2, v2,
                n_t, gtmp, gsend, r1, s2f, s2, r2, fin,
                sem_a, sem_b, sem_g, sem_1, sem_2, sem_3):
    c = lax.axis_index("cell")
    b = lax.axis_index("brick")
    partner = c + 1 - 2 * lax.rem(c, 2)
    loads = []
    for i, (src, dst) in enumerate((
            (master_h, master), (feat_h, feat), (spec_h, spec), (table_h, table), (gain_h, gain), (sends_h, sends),
            (nbr_h, nbr), (cnt_h, cnt), (dist_h, dist), (decay_h, decay), (readout_h, readout), (target_h, target))):
        cp = pltpu.make_async_copy(src, dst, sem_in.at[i])
        cp.start()
        loads.append(cp)
    barrier = pltpu.get_barrier_semaphore()
    low = lax.rem(c, 16)
    base = c - low
    other = 16 - base

    def at(dz, flip):
        return lax.rem(low + 2 * dz + 16, 16) + (other if flip else base)

    def column(flip):
        return b + 1 - 2 * lax.rem(b, 2) if flip else b

    spots = [(1, 0), (1, 1), (2, 0), (2, 1), (-1, 0), (-1, 1), (-2, 0), (-2, 1), (0, 1)]
    hops = [(2, -1, 0), (2, -1, 1), (2, -2, 0), (2, -2, 1), (-2, 1, 0), (-2, 1, 1)]

    def plane(i):
        return peer(at(0, i // 8), lax.rem(b + i % 8, BRICKS))

    for i in range(1, 16):
        pl.semaphore_signal(barrier, inc=1, device_id=plane(i), device_id_type=MESH)
    for dz, flip in spots[:8]:
        pl.semaphore_signal(barrier, inc=1, device_id=peer(at(dz, flip), column(flip)), device_id_type=MESH)
    pl.semaphore_signal(barrier, inc=1, device_id=peer(partner, b), device_id_type=MESH)
    for dz in (2, -2):
        across = at(dz, 0) + 1 - 2 * lax.rem(c, 2)
        pl.semaphore_signal(barrier, inc=1, device_id=peer(across, b), device_id_type=MESH)
    loads[0].wait()
    wa[c] = master[0:2].reshape(16, C).astype(bf16)
    wb[c] = master[2:4].reshape(16, C).astype(bf16)
    pl.semaphore_wait(barrier, 26)

    def send(w, sem, half, i, block, cell, brick):
        cp = pltpu.make_async_remote_copy(
            src_ref=w.at[block], dst_ref=w.at[block], send_sem=sem.at[half, i], recv_sem=sem.at[half + 1, i],
            device_id=peer(cell, brick), device_id_type=MESH)
        cp.start()
        return cp

    def share(w, sem, i, block):
        return send(w, sem, 2, i, block, partner, b)

    def start_near(w, sem):
        near = [send(w, sem, 0, i, c, at(dz, flip), column(flip)) for i, (dz, flip) in enumerate(spots)]
        return near, [share(w, sem, 15, c)]

    def relay(w, sem, near, shared, cross):
        far = []
        for i, (dz, flip) in enumerate(spots):
            near[i].wait_recv()
            block = at(-dz, flip)
            for j, (to, off, kind) in enumerate(hops):
                if (-dz, flip) == (off, kind):
                    far.append(send(w, sem, 0, 9 + j, block, at(to, 0), b))
                    if cross:
                        shared.append(send(w, sem, 2, 9 + j, block, at(to, 0) + 1 - 2 * lax.rem(c, 2), b))
            shared.append(share(w, sem, i, block))
        return far

    def finish(w, sem, far, shared, cross):
        for j, (to, off, kind) in enumerate(hops):
            far[j].wait_recv()
            if not cross:
                shared.append(share(w, sem, 9 + j, at(off - to, kind)))

    near_a, shared_a = start_near(wa, sem_a)
    for cp in loads[1:6]:
        cp.wait()
    eye = lax.broadcasted_iota(jnp.int32, (A, A), 0) == lax.broadcasted_iota(jnp.int32, (A, A), 1)
    col = jnp.sum(jnp.where(eye, jnp.broadcast_to(spec[...], (A, A)), 0).astype(f32), axis=1, keepdims=True)
    e = feat[...].astype(f32)
    tab = table[...].astype(f32)
    add = jnp.zeros((A, C), f32)
    for s in range(4):
        add = jnp.where(col == float(s), tab[s : s + 1, :], add)
    e = e + add
    emb[...] = e
    rms = lax.rsqrt(jnp.sum(e * e, axis=1, keepdims=True) * (1.0 / C) + epsilon_norm)
    n = (e * rms * gain[...]).astype(bf16)
    nt[0:A, :] = n
    row_id = lax.broadcasted_iota(jnp.int32, (A, 32), 0)
    for d in range(BRICKS):
        take = (row_id == sends[d : d + 1, :]).astype(f32).astype(bf16)
        parcel[d] = dot(take, n, TN).astype(bf16)
    nt[pl.ds(pl.multiple_of(A + 32 * b, 32), 32), :] = parcel[b]
    ghosts = []
    for d in range(1, BRICKS):
        to = lax.rem(b + d, BRICKS)
        cp = pltpu.make_async_remote_copy(
            src_ref=parcel.at[to],
            dst_ref=nt.at[pl.ds(pl.multiple_of(A + 32 * b, 32), 32), :],
            send_sem=sem_g.at[0, d], recv_sem=sem_g.at[1, d],
            device_id=peer(c, to), device_id_type=MESH)
        cp.start()
        ghosts.append(cp)
    near_b, shared_b = start_near(wb, sem_b)
    for cp in loads[6:]:
        cp.wait()

    scale = 1.0 / math.sqrt(C // H)
    rows = A * H
    slot = lax.broadcasted_iota(jnp.int32, (K, A), 0)
    masked = jnp.where(slot < cnt[...], nbr[...], 512)
    m_t = masked.T
    d_t = dist[...].T
    m2 = jnp.concatenate([m_t, m_t], axis=1)
    d2 = jnp.concatenate([d_t, d_t], axis=1)
    msk[...] = jnp.bitwise_and(masked, 127)
    for h in range(H):
        idx[pl.ds(h, A, stride=8), :] = m2
        dst8[pl.ds(h, A, stride=8), :] = d2
    far_a = relay(wa, sem_a, near_a, shared_a, True)
    far_b = relay(wb, sem_b, near_b, shared_b, False)
    lane64 = lax.broadcasted_iota(jnp.int32, (K, 128), 1)

    @pl.loop(0, A // 4)
    def _(g):
        for i in range(4):
            column_a = jnp.take_along_axis(msk[...], jnp.full((K, 128), 4 * g + i, jnp.int32), axis=1)
            onehot[g, 64 * i : 64 * i + 64, :] = jnp.where(column_a == lane64, 1.0, 0.0).astype(bf16)

    finish(wa, sem_a, far_a, shared_a, True)
    for cp in ghosts:
        cp.wait()
    n_cols = nt[...].astype(f32).T.astype(bf16)
    n_t[:, 0:T] = n_cols
    n_t[:, T : 2 * T] = n_cols
    for cp in shared_a:
        cp.wait_recv()

    def weight(w, m):
        return w[:, 8 * m : 8 * m + 8, :].astype(f32).reshape(C, C).astype(bf16)

    n_all = nt[...]
    n_own = nt[0:A, :]
    q = dot(n_own, weight(wa, 0), NN).astype(bf16)
    k = dot(n_all, weight(wa, 1), NN).astype(bf16)

    head_of_lane = lax.broadcasted_iota(jnp.int32, (rows, C), 1) // 32
    head_of_row = lax.rem(lax.broadcasted_iota(jnp.int32, (rows, C), 0), 8)
    head_mask = head_of_lane == head_of_row

    def spread_heads(x32):
        for h in range(H):
            rep[pl.ds(h, A, stride=8), :] = x32[:, 0:128]
            rep[pl.ds(rows + h, A, stride=8), :] = x32[:, 128:256]
        x = jnp.concatenate([rep[0:rows, :], rep[rows : 2 * rows, :]], axis=1)
        return jnp.where(head_mask, x, 0.0).astype(bf16)

    qm[...] = spread_heads(q.astype(f32))
    qm_t[...] = qm[...].T
    big[...] = dot(qm[...], k, NT)
    finish(wb, sem_b, far_b, shared_b, False)

    lane = lax.broadcasted_iota(jnp.int32, (128, 128), 1)
    row_in = lax.broadcasted_iota(jnp.int32, (128, 128), 0)
    sub_head = lax.rem(row_in, 8)
    dec = jnp.zeros((128, 128), f32)
    for h in range(H):
        dec = jnp.where(sub_head == h, decay[:, h : h + 1], dec)
    diag = lax.rem(row_in // 8, 2) == lane // 64

    def pick(s):
        r0 = s * 128
        ix = idx[pl.ds(r0, 128), :]
        low = jnp.bitwise_and(ix, 127)
        res = jnp.zeros((128, 128), f32)
        for t in range(3):
            g = jnp.take_along_axis(big[pl.ds(r0, 128), 128 * t : 128 * t + 128], low, axis=1)
            res = jnp.where(ix >= 128 * t, g, res)
        return res, ix < 512

    blank = jnp.zeros((16, 128), bf16)

    def scatter(s, w32):
        kept = jnp.where(diag, w32, 0.0)
        block = idx[128 * s : 128 * s + 128, :] // 128
        parts = [jnp.where(block == t, kept, 0.0).astype(bf16) for t in range(3)]
        dense = []
        for i in range(4):
            r = 32 * i
            left = jnp.concatenate([x[r : r + 16, :] if y == 0 else blank for x in parts for y in range(2)], axis=0)
            right = jnp.concatenate([blank if y == 0 else x[r + 16 : r + 32, :] for x in parts for y in range(2)], axis=0)
            dense.append(dot(jnp.concatenate([left, right], axis=1), onehot[4 * s + i], NN))
        for t in range(3):
            x = jnp.concatenate([d[32 * t : 32 * t + 32, :] for d in dense], axis=0)
            hi, lo = split(x)
            p2[128 * s : 128 * s + 128, 128 * t : 128 * t + 128] = hi
            p2[128 * s : 128 * s + 128, T + 128 * t : T + 128 * t + 128] = lo

    for s in range(8):
        r0 = s * 128
        got, ok = pick(s)
        score = got * scale - dec * dst8[pl.ds(r0, 128), :]
        score = jnp.where(ok, score, -1e30)
        top = jnp.max(score, axis=1, keepdims=True)
        ex = jnp.where(ok, jnp.exp(score - top), 0.0)
        a = ex / (jnp.sum(ex, axis=1, keepdims=True) * 0.5)
        att[pl.ds(r0, 128), :] = a
        scatter(s, a)

    for cp in shared_b:
        cp.wait_recv()
    w_o = weight(wb, 1)
    v = dot(n_all, weight(wb, 0), NN).astype(bf16)

    collect = (lax.broadcasted_iota(jnp.int32, (A, rows), 1) // 8
               == lax.broadcasted_iota(jnp.int32, (A, rows), 0)).astype(f32).astype(bf16)

    def gather_heads(source, mult):
        full = dot(p2[...], source[...], NN)
        if mult is not None:
            full = full * mult
        kept = jnp.where(head_mask, full, 0.0).astype(bf16)
        return dot(collect, kept, NN).astype(bf16)

    v2[0:T, :] = v
    v2[T : 2 * T, :] = v
    k2[0:T, :] = k
    k2[T : 2 * T, :] = k
    attended = gather_heads(v2, None)
    updated = emb[...] + dot(attended, w_o, NN)
    sig = jax.nn.sigmoid(updated)
    e_col = jnp.sum(readout[...] * (updated * sig), axis=1, keepdims=True)
    energy[...] = jnp.sum(jnp.where(eye, e_col, 0.0), axis=0, keepdims=True)
    t_col = jnp.sum(jnp.where(eye, target[...], 0.0), axis=1, keepdims=True)
    grad_energy = loss_weight * (e_col - t_col)
    slope = sig * (1.0 + updated * (1.0 - sig))
    grad_updated = (grad_energy * readout[...] * slope).astype(bf16)
    grad_att = dot(grad_updated, w_o, NT).astype(bf16)

    first = [None] * 4

    def put(m, x):
        gtmp[0:C, :] = x[:, 0:128]
        gtmp[C : 2 * C, :] = x[:, 128:256]
        for d in range(BRICKS):
            gsend[m, d] = jnp.concatenate(
                [gtmp[pl.ds(d, CELLS, stride=8), :], gtmp[pl.ds(C + d, CELLS, stride=8), :]], axis=1).astype(bf16)
        made = []
        for i in range(1, 16):
            half = pl.ds(pl.multiple_of(other if i // 8 else base, 16), 16)
            cp = pltpu.make_async_remote_copy(
                src_ref=gsend.at[m, lax.rem(b + i % 8, BRICKS), half, :], dst_ref=r1.at[m, base // 2 + b],
                send_sem=sem_1.at[m, 0, i], recv_sem=sem_1.at[m, 1, i],
                device_id=plane(i), device_id_type=MESH)
            cp.start()
            made.append(cp)
        first[m] = made

    put(3, dot(attended, grad_updated, TN))
    gm[...] = spread_heads(grad_att.astype(f32))
    gm_t[...] = gm[...].T
    big[...] = dot(gm[...], v, NT)

    def table_grad(rows_t, mult):
        both = dot(rows_t, p2[...], NN)
        tg = both[:, 0:T] + both[:, T : 2 * T]
        if mult is not None:
            tg = tg * mult
        return dot(n_t[...], jnp.concatenate(split(tg), axis=1), NT)

    put(2, table_grad(gm_t[...], None))

    for s in range(8):
        r0 = s * 128
        gw, ok = pick(s)
        a = att[pl.ds(r0, 128), :]
        mean = jnp.sum(a * gw, axis=1, keepdims=True) * 0.5
        scatter(s, a * (gw - mean))

    put(1, table_grad(qm_t[...], scale))
    grad_query = gather_heads(k2, scale)
    put(0, dot(n_t[:, 0:A], grad_query, NN))

    for m in (3, 2, 1, 0):
        total = gsend[m, b, pl.ds(pl.multiple_of(base, 16), 16), :].astype(f32)
        for i in range(1, 16):
            first[m][i - 1].wait_recv()
            source = (other if i // 8 else base) // 2 + lax.rem(b - i % 8 + BRICKS, BRICKS)
            total = total + r1[m, source].astype(f32)
        s2f[pl.ds(2 * m, 16, stride=8), :] = total[:, 0:128]
        s2f[pl.ds(2 * m + 1, 16, stride=8), :] = total[:, 128:256]
    s2[...] = s2f[...].reshape(16, 8, 128).astype(bf16)

    second = []
    for k in range(1, 16):
        to = lax.rem(low + k, 16)
        cp = pltpu.make_async_remote_copy(
            src_ref=s2.at[to], dst_ref=r2.at[low], send_sem=sem_2.at[0, k], recv_sem=sem_2.at[1, k],
            device_id=peer(base + to, b), device_id_type=MESH)
        cp.start()
        second.append(cp)
    r2[low] = s2[low]
    for cp in near_a + near_b + far_a + far_b + shared_a + shared_b:
        cp.wait_send()
    for m in range(4):
        for cp in first[m]:
            cp.wait_send()
    for cp in second:
        cp.wait_recv()
    mine = pl.ds(pl.multiple_of(8 * b, 8), 8)
    fin[mine, :] = jnp.sum(r2[...].astype(f32), axis=0)

    third = []
    for d in range(1, BRICKS):
        cp = pltpu.make_async_remote_copy(
            src_ref=fin.at[mine, :], dst_ref=fin.at[mine, :], send_sem=sem_3.at[0, d], recv_sem=sem_3.at[1, d],
            device_id=peer(c, lax.rem(b + d, BRICKS)), device_id_type=MESH)
        cp.start()
        third.append(cp)
    for cp in second:
        cp.wait_send()
    for cp in third:
        cp.wait()
    for m in range(4):
        out[m] = jnp.concatenate([fin[pl.ds(2 * m, 8, stride=8), :], fin[pl.ds(2 * m + 1, 8, stride=8), :]], axis=1)


def step(*args):
    vm = pl.BlockSpec(memory_space=pltpu.VMEM)
    rows = A * H
    dma = pltpu.SemaphoreType.DMA
    return pl.pallas_call(
        step_kernel,
        out_shape=(pltpu.VMEM((1, A), f32), pltpu.VMEM((4, 8, C), f32)),
        in_specs=[pl.BlockSpec(memory_space=pl.ANY)] * 12,
        out_specs=(vm, vm),
        scratch_shapes=[
            pltpu.VMEM((4, 8, C), f32),
            pltpu.VMEM((A, C), bf16),
            pltpu.VMEM((1, A), jnp.int32),
            pltpu.VMEM((4, C), bf16),
            pltpu.VMEM((1, C), f32),
            pltpu.VMEM((BRICKS, 32), jnp.int32),
            pltpu.VMEM((K, A), jnp.int32),
            pltpu.VMEM((1, A), jnp.int32),
            pltpu.VMEM((K, A), f32),
            pltpu.VMEM((1, H), f32),
            pltpu.VMEM((1, C), f32),
            pltpu.VMEM((1, A), f32),
            dma((12,)),
            pltpu.VMEM((A, C), f32),
            pltpu.VMEM((T, C), bf16),
            pltpu.VMEM((CELLS, 16, C), bf16),
            pltpu.VMEM((CELLS, 16, C), bf16),
            pltpu.VMEM((BRICKS, 32, C), bf16),
            pltpu.VMEM((rows, 128), jnp.int32),
            pltpu.VMEM((rows, 128), f32),
            pltpu.VMEM((2 * rows, 128), f32),
            pltpu.VMEM((rows, C), bf16),
            pltpu.VMEM((rows, C), bf16),
            pltpu.VMEM((C, rows), bf16),
            pltpu.VMEM((C, rows), bf16),
            pltpu.VMEM((rows, T), f32),
            pltpu.VMEM((rows, 128), f32),
            pltpu.VMEM((A // 4, 256, 128), bf16),
            pltpu.VMEM((rows, 2 * T), bf16),
            pltpu.VMEM((K, A), jnp.int32),
            pltpu.VMEM((2 * T, C), bf16),
            pltpu.VMEM((2 * T, C), bf16),
            pltpu.VMEM((C, 2 * T), bf16),
            pltpu.VMEM((2 * C, 128), f32),
            pltpu.VMEM((4, BRICKS, CELLS, C), bf16),
            pltpu.VMEM((4, 16, 16, C), bf16),
            pltpu.VMEM((128, 128), f32),
            pltpu.VMEM((16, 8, 128), bf16),
            pltpu.VMEM((16, 8, 128), bf16),
            pltpu.VMEM((BRICKS * 8, 128), f32),
            dma((4, 16)),
            dma((4, 16)),
            dma((2, BRICKS)),
            dma((4, 2, 16)),
            dma((2, 16)),
            dma((2, BRICKS)),
        ],
        compiler_params=pltpu.CompilerParams(collective_id=0, has_side_effects=True),
        name="step",
    )(*args)


def update_kernel(energy, owned, moment, second, energy_out, moment_out, second_out, step_out):
    g = owned[...]
    m = 0.9 * moment[...] + 0.1 * g
    s = 0.999 * second[...] + 0.001 * g * g
    moment_out[...] = m
    second_out[...] = s
    step_out[...] = m / (jnp.sqrt(s) + 1e-08)
    energy_out[...] = energy[...]


def update(energy, owned, moment, second):
    vm = pl.BlockSpec(memory_space=pltpu.VMEM)
    block = jax.ShapeDtypeStruct((4, 8, C), f32)
    energy = pltpu.with_memory_space_constraint(energy, pltpu.VMEM)
    owned = pltpu.with_memory_space_constraint(owned, pltpu.VMEM)
    moment = pltpu.with_memory_space_constraint(moment, pltpu.VMEM)
    second = pltpu.with_memory_space_constraint(second, pltpu.VMEM)
    return pl.pallas_call(
        update_kernel,
        out_shape=(jax.ShapeDtypeStruct((1, A), f32), block, block, block),
        in_specs=[vm] * 4,
        out_specs=(vm,) * 4,
        name="update",
    )(energy, owned, moment, second)


def body(features, species, species_table, neighbours, counts, send_lists, distances,
         head_decay, norm_gain, readout, targets, master, moment, second):
    energy, owned = step(
        master, features.reshape(A, C), species.reshape(1, A), species_table,
        norm_gain.reshape(1, C), send_lists.reshape(BRICKS, 32),
        neighbours.reshape(K, A), counts.reshape(1, A), distances.reshape(K, A),
        head_decay.reshape(1, H), readout.reshape(1, C), targets.reshape(1, A))
    energies, moment_new, second_new, adam_step = update(energy, owned, moment, second)
    return (energies.reshape(1, 1, A), moment_new, second_new, adam_step)


def solution(mesh):
    return jax.shard_map(
        body,
        mesh=mesh,
        in_specs=(
            P("cell", "brick", None, None),
            P("cell", "brick", None),
            P(),
            P("cell", "brick", None, None),
            P("cell", "brick", None),
            P("cell", "brick", None, None),
            P("cell", "brick", None, None),
            P(),
            P(),
            P(),
            P("cell", "brick", None),
            P(None, "cell", None),
            P(None, "cell", None),
            P(None, "cell", None),
        ),
        out_specs=(
            P("cell", "brick", None),
            P(None, "cell", None),
            P(None, "cell", None),
            P(None, "cell", None),
        ),
        check_vma=False,
    )
```
